256 devices in a mesh: row: 32 (over z, y_lo, core), col: 8 (over y_hi, x).
Axes of the slice: x: 4, y: 4 (y_hi: 2, y_lo: 2; y = y_hi * 2 + y_lo), z: 8, core: 2. Of those that a mesh axis runs over, the one named last changes fastest.
Arguments:
- features: bfloat16 [32768, 128], P(('col', 'row')), may hold values from -96 to 96
- weight: bfloat16 [128, 256], replicated, may hold values from -0.5 to 0.5
- bias: float32 [256], replicated, may hold values from -3 to 3
- cotangent: bfloat16 [32768, 256], P(('row', 'col')), may hold values from -6 to 6
- tile_values: bfloat16 [32, 8, 256, 128, 128], P('row', 'col'), may hold values from 0 to 4, as said below
- tile_pos: int32 [32, 8, 2, 256], P('row', 'col'), may hold values from 0 to 31, as said below
- tile_count: int32 [32, 8], P('row', 'col'), may hold values from 0 to 256, as said below
- block_perm: int32 [256], replicated, may hold values from 0 to 255, as said below
Outputs:
- hidden: bfloat16 [32768, 256], P(('row', 'col'))
- weight_grad: float32 [128, 256], replicated
- bias_grad: float32 [256], replicated
The draws below stay inside these ranges and needn't reach their ends.
Inputs may be any that keep to these rules, and one draw needn't show every extreme that they name: `tile_values`: entries are 0 or a weight of at least 0.25; slots t at or beyond tile_count[r, c] belong to no tile. `tile_pos`: entry [r, c, 0, t] is the slot's tile row, below 8, within row block r, and [r, c, 1, t] its tile column, below 32, within column block c, both in the reordered numbering; the slots of one cell hold distinct positions. `tile_count`: every draw has a cell with 256 live slots. `block_perm`: each aligned run of 8 entries is a permutation of that run's own indices.
All inputs are finite; a program needn't handle non-finite values.
Results may differ from the reference program's by a relative error of at most 0.0059.
Values may be sent and summed in bfloat16 or wider, within the bound.
No kernel may reach another device: no remote copies, remote signals or barrier semaphores. Data moves between devices by JAX's collectives and lax.ppermute only.
A program may use at most 64 MiB of HBM per device.

```python
import jax
import jax.numpy as jnp
from jax import lax

TILE = 128
FEAT = 128
HIDDEN_SIZE = 256
ROW_TILES = 8
ROW_BLOCKS = 32
COL_BLOCKS = 8
COL_TILES = 32
MAX_TILES = 256
NODES = 32768


def draw_tile_values(key, part):
    shape = (ROW_BLOCKS, COL_BLOCKS, MAX_TILES, TILE, TILE)
    key_mask, key_level, key_cell = jax.random.split(jax.random.fold_in(key, 11), 3)
    cell_density = jnp.exp(jax.random.uniform(key_cell, (ROW_BLOCKS, COL_BLOCKS, 1, 1, 1), jnp.float32, -2.1202635, 0.0))
    chance = jax.random.uniform(key_mask, shape, jnp.float32, 0.0, 1.0)
    present = (chance < cell_density).astype(jnp.float32)
    levels = jax.random.uniform(key_level, shape, jnp.float32, -1.3862944, 1.3862944)
    return (present * jnp.exp(levels)).astype(jnp.bfloat16)


def draw_tile_pos(key, part):
    cell_keys = jax.random.split(jax.random.fold_in(key, 23), ROW_BLOCKS * COL_BLOCKS)
    positions = jax.vmap(lambda single: jax.random.permutation(single, MAX_TILES))(cell_keys).astype(jnp.int32)
    tile_rows = positions // COL_TILES
    tile_cols = positions % COL_TILES
    stacked = jnp.stack([tile_rows, tile_cols], axis=1)
    return stacked.reshape(ROW_BLOCKS, COL_BLOCKS, 2, MAX_TILES)


def draw_tile_count(key, part):
    key_one, key_two, key_three = jax.random.split(jax.random.fold_in(key, 37), 3)
    cell_total = ROW_BLOCKS * COL_BLOCKS
    first_draw = jax.random.randint(key_one, (cell_total,), 1, MAX_TILES + 1, dtype=jnp.int32)
    second_draw = jax.random.randint(key_two, (cell_total,), 1, MAX_TILES + 1, dtype=jnp.int32)
    counts = first_draw * second_draw // MAX_TILES
    busiest = jax.random.randint(key_three, (), 0, cell_total, dtype=jnp.int32)
    counts = jnp.where(jnp.arange(cell_total, dtype=jnp.int32) == busiest, MAX_TILES, counts)
    return counts.reshape(ROW_BLOCKS, COL_BLOCKS).astype(jnp.int32)


def draw_block_perm(key, part):
    block_keys = jax.random.split(jax.random.fold_in(key, 41), ROW_BLOCKS)
    local_order = jax.vmap(lambda single: jax.random.permutation(single, ROW_TILES))(block_keys).astype(jnp.int32)
    offsets = (jnp.arange(ROW_BLOCKS, dtype=jnp.int32) * ROW_TILES)[:, None]
    return (local_order + offsets).reshape(ROW_BLOCKS * ROW_TILES)


def steps_of(own_key, dims, cuts, low, largest):
    level, own = 1.0, jax.random.fold_in(own_key, 6)
    for position, shards_of in cuts:
        heights = jnp.exp(jax.random.uniform(jax.random.fold_in(own, position), (shards_of,), jnp.float32, low / len(cuts), largest / len(cuts)))
        level = level * jnp.repeat(heights, dims[position] // shards_of).reshape([-1 if axis == position else 1 for axis in range(len(dims))])
    return level


def bell_draw(rng, extent, deviation, bound, shards=(), kind=jnp.bfloat16):
    drawn = deviation * jax.random.normal(rng, extent, jnp.float32)
    if shards:
        drawn = drawn * steps_of(rng, extent, shards, -0.22, 0.18)
    return jnp.clip(drawn, -bound, bound).astype(kind)


def setup_inputs(seed: int = 0) -> dict:
    key_list = jax.random.split(jax.random.key(seed), 9)
    return {
        "features": bell_draw(key_list[0], (NODES, FEAT), 16.0, 96.0, ((0, 256),)),
        "weight": bell_draw(key_list[1], (FEAT, HIDDEN_SIZE), FEAT ** -0.5, 0.5),
        "bias": bell_draw(key_list[2], (HIDDEN_SIZE,), 0.5, 3.0, (), jnp.float32),
        "cotangent": bell_draw(key_list[3], (NODES, HIDDEN_SIZE), 1.0, 6.0, ((0, 256),)),
        "tile_values": draw_tile_values(jax.random.fold_in(key_list[8], 71), 0),
        "tile_pos": draw_tile_pos(jax.random.fold_in(key_list[8], 71), 0),
        "tile_count": draw_tile_count(jax.random.fold_in(key_list[8], 71), 0),
        "block_perm": draw_block_perm(jax.random.fold_in(key_list[8], 71), 0),
    }


def reference(features, weight, bias, cotangent, tile_values, tile_pos, tile_count, block_perm):
    slot_index = jnp.arange(MAX_TILES, dtype=jnp.int32)

    def cell_maps(row_block, col_block):
        positions = tile_pos[row_block, col_block]
        row_local = block_perm[row_block * ROW_TILES + positions[0]] - row_block * ROW_TILES
        col_local = block_perm[col_block * COL_TILES + positions[1]] - col_block * COL_TILES
        is_live = slot_index < tile_count[row_block, col_block]
        return (row_local, col_local, is_live)

    def degree_cell(cell_index):
        row_block = cell_index // COL_BLOCKS
        col_block = cell_index % COL_BLOCKS
        row_local, col_local, is_live = cell_maps(row_block, col_block)
        values = tile_values[row_block, col_block].astype(jnp.float32)
        row_part = lax.optimization_barrier(jnp.sum(values, axis=2))
        col_part = lax.optimization_barrier(jnp.sum(values, axis=1))
        row_part = jnp.where(is_live[:, None], row_part, 0.0).astype(jnp.float32)
        col_part = jnp.where(is_live[:, None], col_part, 0.0).astype(jnp.float32)
        row_sums = jnp.zeros((ROW_TILES, TILE), jnp.float32).at[row_local].add(row_part)
        col_sums = jnp.zeros((COL_TILES, TILE), jnp.float32).at[col_local].add(col_part)
        return (row_sums.reshape(ROW_TILES * TILE), col_sums.reshape(COL_TILES * TILE))
    cells = jnp.arange(ROW_BLOCKS * COL_BLOCKS, dtype=jnp.int32)
    row_sums, col_sums = lax.map(degree_cell, cells)
    row_degree = 1.0 + lax.optimization_barrier(jnp.sum(row_sums.reshape(ROW_BLOCKS, COL_BLOCKS, ROW_TILES * TILE), axis=1)).reshape(NODES)
    col_degree = 1.0 + lax.optimization_barrier(jnp.sum(col_sums.reshape(ROW_BLOCKS, COL_BLOCKS, COL_TILES * TILE), axis=0)).reshape(NODES)
    scaled = (lax.rsqrt(col_degree)[:, None] * features.astype(jnp.float32)).astype(jnp.bfloat16)

    def row_product(row_block):

        def cell_step(running, col_block):
            row_local, col_local, is_live = cell_maps(row_block, col_block)
            values = tile_values[row_block, col_block].astype(jnp.float32)
            values = values * is_live[:, None, None].astype(jnp.float32)
            dense_cell = jnp.zeros((ROW_TILES, COL_TILES, TILE, TILE), jnp.float32).at[row_local, col_local].add(values)
            dense_cell = jnp.transpose(dense_cell, (0, 2, 1, 3)).reshape(ROW_TILES * TILE, COL_TILES * TILE)
            inputs = lax.dynamic_slice_in_dim(scaled, col_block * (COL_TILES * TILE), COL_TILES * TILE, 0).astype(jnp.float32)
            product = jnp.dot(dense_cell, inputs, preferred_element_type=jnp.float32, precision=lax.Precision.HIGHEST)
            return (running + product, None)
        running, _ = lax.scan(cell_step, jnp.zeros((ROW_TILES * TILE, FEAT), jnp.float32), jnp.arange(COL_BLOCKS, dtype=jnp.int32))
        return running
    summed = lax.map(row_product, jnp.arange(ROW_BLOCKS, dtype=jnp.int32)).reshape(NODES, FEAT)
    aggregated = (lax.rsqrt(row_degree)[:, None] * summed).astype(jnp.bfloat16)
    preact = jnp.dot(aggregated, weight, preferred_element_type=jnp.float32) + bias
    logistic = jax.nn.sigmoid(preact)
    hidden = (preact * logistic).astype(jnp.bfloat16)
    preact_grad = (cotangent.astype(jnp.float32) * logistic * (1.0 + preact * (1.0 - logistic))).astype(jnp.bfloat16)
    inverse_root = lax.rsqrt(jnp.float32(NODES))
    weight_grad = jnp.dot(aggregated.T, preact_grad, preferred_element_type=jnp.float32) * inverse_root
    bias_grad = lax.optimization_barrier(jnp.sum(preact_grad.astype(jnp.float32), axis=0)) * inverse_root
    return (hidden, weight_grad, bias_grad)
```

```python
import functools

import jax
import jax.numpy as jnp
from jax import lax
from jax.experimental import pallas as pl
from jax.experimental.pallas import tpu as pltpu
from jax.sharding import Mesh, PartitionSpec as P

ROW = ("z", "y_lo", "core")
COL = ("y_hi", "x")
SAME_CORE_ROW = ("z", "y_lo")
PLANE = ("y_lo", "core", "y_hi", "x")
SWAP = [(0, 1), (1, 0)]
CHUNK = 32
F32 = jnp.float32


def degree_kernel(ids, perm, count, pos, tiles, col_ref, slot_ref, acc):
    step = pl.program_id(0)
    row, col, core = ids[0], ids[1], ids[2]
    live_count = count[0, 0]

    @pl.when(step == 0)
    def _():
        acc[...] = jnp.zeros_like(acc)

        @pl.loop(0, 264)
        def _(n):
            slot_ref[n] = jnp.int32(-1)

    @pl.when(step * CHUNK < live_count)
    def _():
        @pl.loop(0, CHUNK // 8)
        def _(group):
            for u in range(8):
                local = group * 8 + u
                slot = step * CHUNK + local
                own_row = perm[row * 8 + pos[0, slot]] - row * 8
                own_col = perm[col * 32 + pos[1, slot]] - col * 32
                place = (own_col >> 1) + 16 * ((own_col & 1) ^ core)
                live = slot < live_count
                slot_ref[jnp.where(live, own_row * 32 + place, 256)] = slot
                part = jnp.sum(tiles[local].astype(F32).reshape(16, 8, 128), axis=0)
                acc[place] += jnp.where(live, part, 0.0)

    @pl.when(step == pl.num_programs(0) - 1)
    def _():
        col_ref[...] = jnp.sum(acc[...], axis=1)


def degrees(ids, perm, count, pos, packed):
    steps = packed.shape[0] // CHUNK

    def block(step, ids, perm, count, pos):
        last = jnp.maximum(count[0, 0] - 1, 0) // CHUNK
        return (jnp.minimum(step, last), 0, 0)

    return pl.pallas_call(
        degree_kernel,
        grid_spec=pltpu.PrefetchScalarGridSpec(
            num_scalar_prefetch=4,
            grid=(steps,),
            in_specs=[pl.BlockSpec((CHUNK, 128, 128), block)],
            out_specs=[
                pl.BlockSpec((32, 128), lambda step, *_: (0, 0)),
                pl.BlockSpec(memory_space=pltpu.SMEM),
            ],
            scratch_shapes=[pltpu.VMEM((32, 8, 128), F32)],
        ),
        out_shape=[
            jax.ShapeDtypeStruct((32, 128), F32),
            jax.ShapeDtypeStruct((264,), jnp.int32),
        ],
        name="degrees",
    )(ids, perm, count, pos, packed)


def product_kernel(slots, deg, feat_a, feat_b, *refs):
    tiles, (out, rhs) = refs[:32], refs[32:]
    i = pl.program_id(0)

    @pl.when(i == 0)
    def _():
        scale = jnp.concatenate([lax.rsqrt(1.0 + deg[...]), jnp.zeros((96, 128), F32)], axis=0).T
        for b in range(32):
            feat = feat_a[b] if b < 16 else feat_b[b - 16]
            scaled = scale[:, b : b + 1] * feat.astype(F32)
            rhs[pl.ds(b * 128, 128), 0:128] = scaled.astype(jnp.bfloat16)
            rhs[pl.ds(b * 128, 128), 128:256] = jnp.ones((128, 128), jnp.bfloat16)

    parts = []
    for q in range(32):
        live = slots[i * 32 + q] >= 0
        parts.append(jnp.where(live, tiles[q][0], jnp.zeros((), jnp.bfloat16)))
    lhs = jnp.concatenate(parts, axis=1)
    both = jnp.dot(lhs, rhs[...], preferred_element_type=F32)
    out[0, 0:128, :] = both[:, 0:128]
    out[0, 128:136, :] = both[:, 128:256].T[0:8, :]


def product(slots, deg, feat_a, feat_b, packed):
    def block(q, i, slots):
        return (jnp.maximum(slots[i * 32 + q], 0), 0, 0)

    whole = pl.BlockSpec((16, 128, 128), lambda i, slots: (0, 0, 0))
    return pl.pallas_call(
        product_kernel,
        grid_spec=pltpu.PrefetchScalarGridSpec(
            num_scalar_prefetch=1,
            grid=(8,),
            in_specs=[pl.BlockSpec((32, 128), lambda i, slots: (0, 0)), whole, whole]
            + [pl.BlockSpec((1, 128, 128), functools.partial(block, q)) for q in range(32)],
            out_specs=pl.BlockSpec((1, 136, 128), lambda i, slots: (i, 0, 0)),
            scratch_shapes=[pltpu.VMEM((4096, 256), jnp.bfloat16)],
        ),
        out_shape=jax.ShapeDtypeStruct((8, 136, 128), F32),
        name="product",
    )(slots, deg, feat_a, feat_b, *([packed] * 32))


def node_kernel(parts, weight, bias, cotangent, hidden_ref, terms_ref):
    total = jnp.sum(parts[...], axis=0)
    row_degree = jnp.broadcast_to(1.0 + total[128:129, :], (128, 128)).T
    aggregated = (lax.rsqrt(row_degree) * total[0:128, :]).astype(jnp.bfloat16)
    preact = jnp.dot(aggregated, weight[...], preferred_element_type=F32) + bias[...]
    logistic = jax.nn.sigmoid(preact)
    hidden_ref[...] = (preact * logistic).astype(jnp.bfloat16)
    grad = (
        cotangent[...].astype(F32) * logistic * (1.0 + preact * (1.0 - logistic))
    ).astype(jnp.bfloat16)
    weight_part = lax.dot_general(
        aggregated, grad, (((0,), (0,)), ((), ())), preferred_element_type=F32
    )
    bias_part = jnp.sum(grad.astype(F32), axis=0, keepdims=True)
    for k in range(32):
        half, f = k // 16, (k % 16) * 8
        for s in range(8):
            terms_ref[k, s, :, :] = weight_part[f + s : f + s + 1, half * 128 : half * 128 + 128]
        terms_ref[k, 8, :, :] = (
            bias_part[:, k * 128 : k * 128 + 128] if k < 2 else jnp.zeros((1, 128), F32)
        )


def nodes(parts, weight, bias, cotangent):
    return pl.pallas_call(
        node_kernel,
        out_shape=[
            jax.ShapeDtypeStruct((128, 256), jnp.bfloat16),
            jax.ShapeDtypeStruct((32, 9, 1, 128), F32),
        ],
        name="nodes",
    )(parts, weight, bias, cotangent)


def gather(x, axes, count):
    return lax.all_to_all(jnp.broadcast_to(x[None], (count,) + x.shape), axes, 0, 0)


def body(features, weight, bias, cotangent, tile_values, tile_pos, tile_count, block_perm):
    packed = tile_values[0, 0]
    ids = jnp.stack([lax.axis_index(ROW), lax.axis_index(COL), lax.axis_index("core")])
    feat_a = gather(features, SAME_CORE_ROW, 16)
    col_part, slots = degrees(ids, block_perm, tile_count, tile_pos[0, 0], packed)
    col_half = col_part[:16] + lax.ppermute(col_part[16:], "core", SWAP)
    deg_a = jnp.sum(gather(col_half, SAME_CORE_ROW, 16), axis=0)
    deg_b = lax.ppermute(deg_a, "core", SWAP)
    feat_b = lax.ppermute(feat_a, "core", SWAP)
    partial = product(slots, jnp.concatenate([deg_a, deg_b]), feat_a, feat_b, packed)
    received = lax.all_to_all(partial, COL, 0, 0)
    hidden, terms = nodes(received, weight, bias[None], cotangent)
    own_terms = jnp.sum(lax.all_to_all(terms, PLANE, 0, 0), axis=0)
    total = jnp.sum(gather(own_terms, ("z",), 8), axis=0) * lax.rsqrt(F32(32768.0))
    every = gather(total, PLANE, 32)[:, :, 0, :]
    weight_rows = every[:, :8, :].reshape(2, 128, 128)
    weight_grad = jnp.concatenate([weight_rows[0], weight_rows[1]], axis=1)
    return hidden, weight_grad, every[:2, 8, :].reshape(256)


def solution(mesh):
    split = Mesh(mesh.devices.reshape(8, 2, 2, 2, 4), ("z", "y_lo", "core", "y_hi", "x"))
    placed = (
        P(COL + ROW, None),
        P(),
        P(),
        P(ROW + COL, None),
        P(ROW, COL, None, None, None),
        P(ROW, COL, None, None),
        P(ROW, COL),
        P(),
    )
    return jax.shard_map(
        body,
        mesh=split,
        in_specs=placed,
        out_specs=(P(ROW + COL, None), P(), P()),
        check_vma=False,
    )
```

```python
import functools

import jax
import jax.numpy as jnp
from jax import lax
from jax.experimental import pallas as pl
from jax.experimental.pallas import tpu as pltpu
from jax.sharding import Mesh, PartitionSpec as P

ROW = ("z", "y_lo", "core")
COL = ("y_hi", "x")
SAME_CORE_ROW = ("z", "y_lo")
PLANE = ("y_lo", "core", "y_hi", "x")
SWAP = [(0, 1), (1, 0)]
CHUNK = 32
F32 = jnp.float32
BF16 = jnp.bfloat16


def degree_kernel(count, perm, pos, feats, tiles, send_ref, slot_ref, sums):
    step = pl.program_id(0)
    live_count = count[0, 0]

    @pl.when(step * CHUNK < live_count)
    def _():
        for group in range(CHUNK // 8):
            rows = []
            for u in range(8):
                tile = tiles[group * 8 + u].astype(F32)
                rows.append(jnp.sum(tile, axis=0, keepdims=True))
            sums[pl.ds(step * CHUNK + group * 8, 8), :] = jnp.concatenate(rows, axis=0)

    @pl.when(step * CHUNK >= live_count)
    def _():
        sums[pl.ds(step * CHUNK, CHUNK), :] = jnp.zeros((CHUNK, 128), F32)

    @pl.when(step == pl.num_programs(0) - 1)
    def _():
        row, col, core = lax.axis_index(ROW), lax.axis_index(COL), lax.axis_index("core")
        own_row = jnp.zeros((1, 256), jnp.int32)
        own_col = jnp.zeros((1, 256), jnp.int32)
        for v in range(8):
            own_row += jnp.where(pos[0:1, :] == v, perm[row * 8 + v] - row * 8, 0)
        for v in range(32):
            own_col += jnp.where(pos[1:2, :] == v, perm[col * 32 + v] - col * 32, 0)
        place = (own_col >> 1) + 16 * ((own_col & 1) ^ core)
        slot = lax.broadcasted_iota(jnp.int32, (1, 256), 1)
        live = slot < live_count
        place = jnp.where(live, place, 512)
        dense = own_row * 32 + place
        pick = (lax.broadcasted_iota(jnp.int32, (32, 256), 0) == place).astype(F32)
        col_part = jnp.dot(
            pick, sums[...], precision=lax.Precision.HIGHEST, preferred_element_type=F32
        ).astype(BF16)
        match = lax.broadcasted_iota(jnp.int32, (256, 256), 0) == dense
        number = lax.broadcasted_iota(jnp.int32, (16, 256), 1) + 1
        found = lax.dot_general(
            number.astype(F32).astype(BF16),
            match.astype(F32).astype(BF16),
            (((1,), (1,)), ((), ())),
            preferred_element_type=F32,
        )
        slot_ref[...] = found[0:1, :].astype(jnp.int32) - 1
        for m in range(16):
            send_ref[m, 0:128, :] = feats[...]
            send_ref[m, 128:160, :] = col_part


def degrees(count, perm, pos, features, packed):
    steps = packed.shape[0] // CHUNK

    def block(step, count, perm):
        last = jnp.maximum(count[0, 0] - 1, 0) // CHUNK
        return (jnp.minimum(step, last), 0, 0)

    return pl.pallas_call(
        degree_kernel,
        grid_spec=pltpu.PrefetchScalarGridSpec(
            num_scalar_prefetch=2,
            grid=(steps,),
            in_specs=[
                pl.BlockSpec((2, 256), lambda step, *_: (0, 0)),
                pl.BlockSpec((128, 128), lambda step, *_: (0, 0)),
                pl.BlockSpec((CHUNK, 128, 128), block),
            ],
            out_specs=[
                pl.BlockSpec((16, 160, 128), lambda step, *_: (0, 0, 0)),
                pl.BlockSpec((1, 256), lambda step, *_: (0, 0)),
            ],
            scratch_shapes=[pltpu.VMEM((256, 128), F32)],
        ),
        out_shape=[
            jax.ShapeDtypeStruct((16, 160, 128), BF16),
            jax.ShapeDtypeStruct((1, 256), jnp.int32),
        ],
        compiler_params=pltpu.CompilerParams(vmem_limit_bytes=16 << 20),
        name="degrees",
    )(count, perm, pos, features, packed)


def product_kernel(slots, recv_a, recv_b, tiles, out, rhs, acc):
    from_a = jnp.sum(recv_a[:, 128:160, :].astype(F32), axis=0)
    from_b = jnp.sum(recv_b[:, 128:160, :].astype(F32), axis=0)
    degree = 1.0 + from_a + jnp.concatenate([from_b[16:32], from_b[0:16]], axis=0)
    scale = jnp.concatenate([lax.rsqrt(degree), jnp.zeros((96, 128), F32)], axis=0).T
    for b in range(32):
        feat = recv_a[b, 0:128, :] if b < 16 else recv_b[b - 16, 0:128, :]
        scaled = scale[:, b : b + 1] * feat.astype(F32)
        rhs[pl.ds(b * 128, 128), 0:128] = scaled.astype(BF16)
    rhs[:, 128:256] = jnp.ones((4096, 128), BF16)
    acc[...] = jnp.zeros_like(acc)

    @pl.loop(0, 8)
    def _(s):
        rows = []
        for i in range(8):
            parts = []
            for q in range(4):
                slot = slots[0, i * 32 + s * 4 + q]
                tile = tiles[jnp.maximum(slot, 0)]
                parts.append(jnp.where(slot >= 0, tile, jnp.zeros((), BF16)))
            rows.append(jnp.concatenate(parts, axis=1))
        lhs = jnp.concatenate(rows, axis=0)
        acc[...] += jnp.dot(
            lhs, rhs[pl.ds(pl.multiple_of(s * 512, 512), 512), :], preferred_element_type=F32
        )

    for i in range(8):
        out[i, 0:128, :] = acc[i * 128 : i * 128 + 128, 0:128].astype(BF16)
        sums = acc[i * 128 : i * 128 + 128, 128:256].T[0:8, :]
        high = sums.astype(BF16)
        low = (sums - high.astype(F32)).astype(BF16)
        out[i, 128:144, :] = jnp.concatenate([high, low], axis=0)


def product(slots, recv_a, recv_b, packed):
    vmem = pl.BlockSpec(memory_space=pltpu.VMEM)
    return pl.pallas_call(
        product_kernel,
        in_specs=[pl.BlockSpec(memory_space=pltpu.SMEM), vmem, vmem, vmem],
        out_specs=vmem,
        scratch_shapes=[pltpu.VMEM((4096, 256), BF16), pltpu.VMEM((1024, 256), F32)],
        out_shape=jax.ShapeDtypeStruct((8, 144, 128), BF16),
        compiler_params=pltpu.CompilerParams(vmem_limit_bytes=24 << 20),
        name="product",
    )(slots, recv_a, recv_b, packed)


def node_kernel(parts, weight, bias, cotangent, hidden_ref, terms_ref):
    total = jnp.sum(parts[...].astype(F32), axis=0)
    row_degree = jnp.broadcast_to(1.0 + total[128:129, :] + total[136:137, :], (128, 128)).T
    aggregated = (lax.rsqrt(row_degree) * total[0:128, :]).astype(BF16)
    preact = jnp.dot(aggregated, weight[...], preferred_element_type=F32) + bias[...]
    logistic = jax.nn.sigmoid(preact)
    hidden_ref[...] = (preact * logistic).astype(BF16)
    grad = (
        cotangent[...].astype(F32) * logistic * (1.0 + preact * (1.0 - logistic))
    ).astype(BF16)
    weight_part = lax.dot_general(
        aggregated, grad, (((0,), (0,)), ((), ())), preferred_element_type=F32
    )
    bias_part = jnp.sum(grad.astype(F32), axis=0, keepdims=True)
    for k in range(32):
        half, f = k // 16, (k % 16) * 8
        for s in range(8):
            terms_ref[k, s, :, :] = weight_part[f + s : f + s + 1, half * 128 : half * 128 + 128]
        terms_ref[k, 8, :, :] = (
            bias_part[:, k * 128 : k * 128 + 128] if k < 2 else jnp.zeros((1, 128), F32)
        )


def nodes(parts, weight, bias, cotangent):
    return pl.pallas_call(
        node_kernel,
        out_shape=[
            jax.ShapeDtypeStruct((128, 256), BF16),
            jax.ShapeDtypeStruct((32, 9, 1, 128), F32),
        ],
        compiler_params=pltpu.CompilerParams(vmem_limit_bytes=16 << 20),
        name="nodes",
    )(parts, weight, bias, cotangent)


def gather(x, axes, count):
    return lax.all_to_all(jnp.broadcast_to(x[None], (count,) + x.shape), axes, 0, 0)


def body(features, weight, bias, cotangent, tile_values, tile_pos, tile_count, block_perm):
    packed = tile_values[0, 0]
    streamed = pltpu.with_memory_space_constraint(packed, pltpu.HBM)
    send, slots = degrees(tile_count, block_perm, tile_pos[0, 0], features, streamed)
    recv_a = lax.all_to_all(send, SAME_CORE_ROW, 0, 0)
    recv_b = lax.ppermute(recv_a, "core", SWAP)
    held = pltpu.with_memory_space_constraint(packed, pltpu.VMEM)
    partial = product(slots, recv_a, recv_b, held)
    received = lax.all_to_all(partial, COL, 0, 0)
    hidden, terms = nodes(received, weight, bias[None], cotangent)
    own_terms = jnp.sum(lax.all_to_all(terms, PLANE, 0, 0), axis=0)
    total = jnp.sum(gather(own_terms, ("z",), 8), axis=0) * lax.rsqrt(F32(32768.0))
    every = gather(total, PLANE, 32)[:, :, 0, :]
    weight_rows = every[:, :8, :].reshape(2, 128, 128)
    weight_grad = jnp.concatenate([weight_rows[0], weight_rows[1]], axis=1)
    return hidden, weight_grad, every[:2, 8, :].reshape(256)


def solution(mesh):
    split = Mesh(mesh.devices.reshape(8, 2, 2, 2, 4), ("z", "y_lo", "core", "y_hi", "x"))
    placed = (
        P(COL + ROW, None),
        P(),
        P(),
        P(ROW + COL, None),
        P(ROW, COL, None, None, None),
        P(ROW, COL, None, None),
        P(ROW, COL),
        P(),
    )
    return jax.shard_map(
        body,
        mesh=split,
        in_specs=placed,
        out_specs=(P(ROW + COL, None), P(), P()),
        check_vma=False,
    )
```

```python
import functools

import jax
import jax.numpy as jnp
from jax import lax
from jax.experimental import pallas as pl
from jax.experimental.pallas import tpu as pltpu
from jax.sharding import Mesh, PartitionSpec as P

ROW = ("z", "y_lo", "core")
COL = ("y_hi", "x")
SAME_CORE_ROW = ("z", "y_lo")
PLANE = ("y_lo", "core", "y_hi", "x")
SWAP = [(0, 1), (1, 0)]
CHUNK = 32
F32 = jnp.float32
BF16 = jnp.bfloat16


def degree_kernel(count, perm, pos_hbm, feats_hbm, tiles_hbm, send_ref, slot_ref, tiles, pos, feats, sums, sem, small):
    steps = 256 // CHUNK

    def chunk_copy(step):
        part = pl.ds(step * CHUNK, CHUNK)
        return pltpu.make_async_copy(tiles_hbm.at[part], tiles.at[part], sem.at[step])

    pos_copy = pltpu.make_async_copy(pos_hbm, pos, small.at[0])
    feats_copy = pltpu.make_async_copy(feats_hbm, feats, small.at[1])
    pos_copy.start()
    for step in range(steps):
        chunk_copy(step).start()
    feats_copy.start()
    live_count = count[0, 0]
    row, col, core = lax.axis_index(ROW), lax.axis_index(COL), lax.axis_index("core")
    pos_copy.wait()
    own_row = jnp.zeros((1, 256), jnp.int32)
    own_col = jnp.zeros((1, 256), jnp.int32)
    for v in range(8):
        own_row += jnp.where(pos[0:1, :] == v, perm[row * 8 + v] - row * 8, 0)
    for v in range(32):
        own_col += jnp.where(pos[1:2, :] == v, perm[col * 32 + v] - col * 32, 0)
    place = (own_col >> 1) + 16 * ((own_col & 1) ^ core)
    slot = lax.broadcasted_iota(jnp.int32, (1, 256), 1)
    place = jnp.where(slot < live_count, place, 512)
    dense = own_row * 32 + place
    match = lax.broadcasted_iota(jnp.int32, (256, 256), 0) == dense
    number = lax.broadcasted_iota(jnp.int32, (16, 256), 1) + 1
    found = lax.dot_general(
        number.astype(F32).astype(BF16),
        match.astype(F32).astype(BF16),
        (((1,), (1,)), ((), ())),
        preferred_element_type=F32,
    )
    slot_ref[...] = found[0:1, :].astype(jnp.int32) - 1

    @pl.loop(0, steps)
    def _(step):
        chunk_copy(step).wait()
        base = step * CHUNK

        @pl.when(base < live_count)
        def _():
            for group in range(CHUNK // 8):
                rows = []
                for u in range(8):
                    tile = tiles[base + group * 8 + u].astype(F32)
                    rows.append(jnp.sum(tile, axis=0, keepdims=True))
                sums[pl.ds(base + group * 8, 8), :] = jnp.concatenate(rows, axis=0)

        @pl.when(base >= live_count)
        def _():
            sums[pl.ds(base, CHUNK), :] = jnp.zeros((CHUNK, 128), F32)

    pick = (lax.broadcasted_iota(jnp.int32, (32, 256), 0) == place).astype(F32)
    col_part = jnp.dot(
        pick, sums[...], precision=lax.Precision.HIGHEST, preferred_element_type=F32
    ).astype(BF16)
    feats_copy.wait()
    for m in range(16):
        send_ref[m, 0:128, :] = feats[...]
        send_ref[m, 128:160, :] = col_part


def degrees(count, perm, pos, features, packed):
    smem = pl.BlockSpec(memory_space=pltpu.SMEM)
    vmem = pl.BlockSpec(memory_space=pltpu.VMEM)
    hbm = pl.BlockSpec(memory_space=pltpu.HBM)
    return pl.pallas_call(
        degree_kernel,
        in_specs=[smem, smem, hbm, hbm, hbm],
        out_specs=[vmem, vmem, vmem],
        scratch_shapes=[
            pltpu.VMEM((2, 256), jnp.int32),
            pltpu.VMEM((128, 128), BF16),
            pltpu.VMEM((256, 128), F32),
            pltpu.SemaphoreType.DMA((256 // CHUNK,)),
            pltpu.SemaphoreType.DMA((2,)),
        ],
        out_shape=[
            jax.ShapeDtypeStruct((16, 160, 128), BF16),
            jax.ShapeDtypeStruct((1, 256), jnp.int32),
            pltpu.VMEM((256, 128, 128), BF16),
        ],
        compiler_params=pltpu.CompilerParams(vmem_limit_bytes=16 << 20),
        name="degrees",
    )(count, perm, pos, features, packed)


def arrange_kernel(slots, tiles, dense, sums_ref):
    @pl.loop(0, 8)
    def _(i):
        total = jnp.zeros((128, 128), F32)
        for place in range(32):
            slot = slots[0, i * 32 + place]
            tile = jnp.where(slot >= 0, tiles[jnp.maximum(slot, 0)], jnp.zeros((), BF16))
            rows = pl.ds(pl.multiple_of(i * 128, 128), 128)
            lane = place % 8 * 128
            dense[place // 8, rows, lane : lane + 128] = tile
            total += tile.astype(F32)
        sums = jnp.broadcast_to(jnp.sum(total.T, axis=0, keepdims=True), (8, 128))
        high = sums.astype(BF16)
        low = (sums - high.astype(F32)).astype(BF16)
        sums_ref[i] = jnp.concatenate([high, low], axis=0)


def arrange(slots, tiles):
    vmem = pl.BlockSpec(memory_space=pltpu.VMEM)
    return pl.pallas_call(
        arrange_kernel,
        in_specs=[pl.BlockSpec(memory_space=pltpu.SMEM), vmem],
        out_specs=[vmem, vmem],
        out_shape=[
            pltpu.VMEM((4, 1024, 1024), BF16),
            pltpu.VMEM((8, 16, 128), BF16),
        ],
        cost_estimate=pl.CostEstimate(flops=0, bytes_accessed=16 << 20, transcendentals=0),
        compiler_params=pltpu.CompilerParams(vmem_limit_bytes=16 << 20),
        name="arrange",
    )(slots, tiles)


def product_kernel(recv_a, recv_b, dense, sums, out, rhs, acc):
    from_a = jnp.sum(recv_a[:, 128:160, :].astype(F32), axis=0)
    from_b = jnp.sum(recv_b[:, 128:160, :].astype(F32), axis=0)
    degree = 1.0 + from_a + jnp.concatenate([from_b[16:32], from_b[0:16]], axis=0)
    scale = jnp.concatenate([lax.rsqrt(degree), jnp.zeros((96, 128), F32)], axis=0).T
    for part in range(4):
        for b in range(part * 8, part * 8 + 8):
            feat = recv_a[b, 0:128, :] if b < 16 else recv_b[b - 16, 0:128, :]
            scaled = scale[:, b : b + 1] * feat.astype(F32)
            rhs[b * 128 : b * 128 + 128, :] = scaled.astype(BF16)
        term = jnp.dot(
            dense[part], rhs[part * 1024 : part * 1024 + 1024, :], preferred_element_type=F32
        )
        if part == 0:
            acc[...] = term
        elif part < 3:
            acc[...] += term
        else:
            total = (acc[...] + term).astype(BF16)
    for i in range(8):
        out[i, 0:128, :] = total[i * 128 : i * 128 + 128, :]
        out[i, 128:144, :] = sums[i]


def product(recv_a, recv_b, dense, sums):
    vmem = pl.BlockSpec(memory_space=pltpu.VMEM)
    return pl.pallas_call(
        product_kernel,
        in_specs=[vmem, vmem, vmem, vmem],
        out_specs=vmem,
        scratch_shapes=[pltpu.VMEM((4096, 128), BF16), pltpu.VMEM((1024, 128), F32)],
        out_shape=jax.ShapeDtypeStruct((8, 144, 128), BF16),
        compiler_params=pltpu.CompilerParams(vmem_limit_bytes=24 << 20),
        name="product",
    )(recv_a, recv_b, dense, sums)


def node_kernel(parts, weight, bias, cotangent, hidden_ref, terms_ref):
    total = jnp.sum(parts[...].astype(F32), axis=0)
    row_degree = jnp.broadcast_to(1.0 + total[128:129, :] + total[136:137, :], (128, 128)).T
    aggregated = (lax.rsqrt(row_degree) * total[0:128, :]).astype(BF16)
    preact = jnp.dot(aggregated, weight[...], preferred_element_type=F32) + bias[...]
    logistic = jax.nn.sigmoid(preact)
    hidden_ref[...] = (preact * logistic).astype(BF16)
    grad = (
        cotangent[...].astype(F32) * logistic * (1.0 + preact * (1.0 - logistic))
    ).astype(BF16)
    weight_part = lax.dot_general(
        aggregated, grad, (((0,), (0,)), ((), ())), preferred_element_type=F32
    )
    bias_part = jnp.sum(grad.astype(F32), axis=0, keepdims=True)
    for k in range(32):
        half, f = k // 16, (k % 16) * 8
        for s in range(8):
            terms_ref[k, s, :, :] = weight_part[f + s : f + s + 1, half * 128 : half * 128 + 128]
        terms_ref[k, 8, :, :] = (
            bias_part[:, k * 128 : k * 128 + 128] if k < 2 else jnp.zeros((1, 128), F32)
        )


def nodes(parts, weight, bias, cotangent):
    return pl.pallas_call(
        node_kernel,
        out_shape=[
            jax.ShapeDtypeStruct((128, 256), BF16),
            jax.ShapeDtypeStruct((32, 9, 1, 128), F32),
        ],
        compiler_params=pltpu.CompilerParams(vmem_limit_bytes=16 << 20),
        name="nodes",
    )(parts, weight, bias, cotangent)


def finish_kernel(every, weight_ref, bias_ref):
    for k in range(32):
        half, f = k // 16, (k % 16) * 8
        for s in range(8):
            weight_ref[f + s : f + s + 1, half * 128 : half * 128 + 128] = every[k, s, :, :]
    for k in range(2):
        bias_ref[:, k * 128 : k * 128 + 128] = every[k, 8, :, :]


def finish(every):
    return pl.pallas_call(
        finish_kernel,
        out_shape=[
            jax.ShapeDtypeStruct((128, 256), F32),
            jax.ShapeDtypeStruct((1, 256), F32),
        ],
        compiler_params=pltpu.CompilerParams(vmem_limit_bytes=16 << 20),
        name="finish",
    )(every)


def gather(x, axes, count):
    return lax.all_to_all(jnp.broadcast_to(x[None], (count,) + x.shape), axes, 0, 0)


def body(features, weight, bias, cotangent, tile_values, tile_pos, tile_count, block_perm):
    packed = tile_values[0, 0]
    in_hbm = [
        pltpu.with_memory_space_constraint(x, pltpu.HBM)
        for x in (block_perm, tile_pos[0, 0], features, packed)
    ]
    send, slots, held = degrees(tile_count, *in_hbm)
    recv_a = lax.all_to_all(send, SAME_CORE_ROW, 0, 0)
    recv_b = lax.ppermute(recv_a, "core", SWAP)
    partial = product(recv_a, recv_b, *arrange(slots, held))
    received = lax.all_to_all(partial, COL, 0, 0)
    hidden, terms = nodes(received, weight, bias[None], cotangent)
    own_terms = jnp.sum(lax.all_to_all(terms, PLANE, 0, 0), axis=0)
    total = jnp.sum(gather(own_terms, ("z",), 8), axis=0) * lax.rsqrt(F32(32768.0))
    weight_grad, bias_grad = finish(gather(total, PLANE, 32))
    return hidden, weight_grad, bias_grad[0]


def solution(mesh):
    split = Mesh(mesh.devices.reshape(8, 2, 2, 2, 4), ("z", "y_lo", "core", "y_hi", "x"))
    placed = (
        P(COL + ROW, None),
        P(),
        P(),
        P(ROW + COL, None),
        P(ROW, COL, None, None, None),
        P(ROW, COL, None, None),
        P(ROW, COL),
        P(),
    )
    return jax.shard_map(
        body,
        mesh=split,
        in_specs=placed,
        out_specs=(P(ROW + COL, None), P(), P()),
        check_vma=False,
    )
```

```python
import functools

import jax
import jax.numpy as jnp
from jax import lax
from jax.experimental import pallas as pl
from jax.experimental.pallas import tpu as pltpu
from jax.sharding import Mesh, PartitionSpec as P

ROW = ("z", "y_lo", "core")
COL = ("y_hi", "x")
SAME_CORE_ROW = ("z", "y_lo")
PLANE = ("y_lo", "core", "y_hi", "x")
SWAP = [(0, 1), (1, 0)]
CHUNK = 16
F32 = jnp.float32
BF16 = jnp.bfloat16


def degree_kernel(count, perm, pos_hbm, feats_hbm, tiles_hbm, send_ref, slot_ref, tiles, pos, feats, sums, sem, small):
    steps = 256 // CHUNK

    def chunk_copy(step):
        part = pl.ds(step * CHUNK, CHUNK)
        return pltpu.make_async_copy(tiles_hbm.at[part], tiles.at[part], sem.at[step])

    pos_copy = pltpu.make_async_copy(pos_hbm, pos, small.at[0])
    feats_copy = pltpu.make_async_copy(feats_hbm, feats, small.at[1])
    pos_copy.start()
    live_count = count[0, 0]
    for step in range(steps):

        @pl.when(step * CHUNK < live_count)
        def _():
            chunk_copy(step).start()

    feats_copy.start()
    row, col, core = lax.axis_index(ROW), lax.axis_index(COL), lax.axis_index("core")
    pos_copy.wait()
    own_row = jnp.zeros((1, 256), jnp.int32)
    own_col = jnp.zeros((1, 256), jnp.int32)
    for v in range(8):
        own_row += jnp.where(pos[0:1, :] == v, perm[row * 8 + v] - row * 8, 0)
    for v in range(32):
        own_col += jnp.where(pos[1:2, :] == v, perm[col * 32 + v] - col * 32, 0)
    place = (own_col >> 1) + 16 * ((own_col & 1) ^ core)
    slot = lax.broadcasted_iota(jnp.int32, (1, 256), 1)
    place = jnp.where(slot < live_count, place, 512)
    dense = own_row * 32 + place
    match = lax.broadcasted_iota(jnp.int32, (256, 256), 0) == dense
    number = lax.broadcasted_iota(jnp.int32, (16, 256), 1) + 1
    found = lax.dot_general(
        number.astype(F32).astype(BF16),
        match.astype(F32).astype(BF16),
        (((1,), (1,)), ((), ())),
        preferred_element_type=F32,
    )
    found = found[0:1, :].astype(jnp.int32)
    slot_ref[...] = jnp.where(found == 0, 256, found - 1)
    tiles[256] = jnp.zeros((128, 128), BF16)

    @pl.loop(0, steps)
    def _(step):
        base = step * CHUNK

        @pl.when(base < live_count)
        def _():
            chunk_copy(step).wait()
            for group in range(CHUNK // 8):
                rows = []
                for u in range(8):
                    tile = tiles[base + group * 8 + u].astype(F32)
                    rows.append(jnp.sum(tile, axis=0, keepdims=True))
                sums[pl.ds(base + group * 8, 8), :] = jnp.concatenate(rows, axis=0)

        @pl.when(base >= live_count)
        def _():
            sums[pl.ds(base, CHUNK), :] = jnp.zeros((CHUNK, 128), F32)

    pick = (lax.broadcasted_iota(jnp.int32, (32, 256), 0) == place).astype(F32).astype(BF16)
    high = sums[...].astype(BF16)
    low = (sums[...] - high.astype(F32)).astype(BF16)
    col_part = jnp.dot(pick, high, preferred_element_type=F32)
    col_part += jnp.dot(pick, low, preferred_element_type=F32)
    feats_copy.wait()
    for m in range(16):
        send_ref[m, 0:128, :] = feats[...]
        send_ref[m, 128:160, :] = col_part.astype(BF16)


def degrees(count, perm, pos, features, packed):
    smem = pl.BlockSpec(memory_space=pltpu.SMEM)
    vmem = pl.BlockSpec(memory_space=pltpu.VMEM)
    hbm = pl.BlockSpec(memory_space=pltpu.HBM)
    return pl.pallas_call(
        degree_kernel,
        in_specs=[smem, smem, hbm, hbm, hbm],
        out_specs=[vmem, vmem, vmem],
        scratch_shapes=[
            pltpu.VMEM((2, 256), jnp.int32),
            pltpu.VMEM((128, 128), BF16),
            pltpu.VMEM((256, 128), F32),
            pltpu.SemaphoreType.DMA((256 // CHUNK,)),
            pltpu.SemaphoreType.DMA((2,)),
        ],
        out_shape=[
            jax.ShapeDtypeStruct((16, 160, 128), BF16),
            jax.ShapeDtypeStruct((1, 256), jnp.int32),
            pltpu.VMEM((257, 128, 128), BF16),
        ],
        compiler_params=pltpu.CompilerParams(vmem_limit_bytes=16 << 20),
        name="degrees",
    )(count, perm, pos, features, packed)


def row_sum_kernel(slots, tiles, sums_ref):
    @pl.loop(0, 8)
    def _(i):
        total = jnp.zeros((128, 128), F32)
        for place in range(32):
            total += tiles[slots[0, i * 32 + place]].astype(F32)
        sums = jnp.broadcast_to(jnp.sum(total.T, axis=0, keepdims=True), (8, 128))
        high = sums.astype(BF16)
        low = (sums - high.astype(F32)).astype(BF16)
        sums_ref[i] = jnp.concatenate([high, low], axis=0)


def row_sums(slots, tiles):
    vmem = pl.BlockSpec(memory_space=pltpu.VMEM)
    return pl.pallas_call(
        row_sum_kernel,
        in_specs=[pl.BlockSpec(memory_space=pltpu.SMEM), vmem],
        out_specs=vmem,
        out_shape=pltpu.VMEM((8, 16, 128), BF16),
        cost_estimate=pl.CostEstimate(flops=0, bytes_accessed=6 << 20, transcendentals=0),
        compiler_params=pltpu.CompilerParams(vmem_limit_bytes=16 << 20),
        name="row_sums",
    )(slots, tiles)


def product_kernel(slots, recv_a, recv_b, tiles, sums, out, rhs, acc):
    from_a = jnp.sum(recv_a[:, 128:160, :].astype(F32), axis=0)
    from_b = jnp.sum(recv_b[:, 128:160, :].astype(F32), axis=0)
    degree = 1.0 + from_a + jnp.concatenate([from_b[16:32], from_b[0:16]], axis=0)
    scale = jnp.concatenate([lax.rsqrt(degree), jnp.zeros((96, 128), F32)], axis=0).T
    for part in range(4):
        for b in range(part * 8, part * 8 + 8):
            feat = recv_a[b, 0:128, :] if b < 16 else recv_b[b - 16, 0:128, :]
            scaled = scale[:, b : b + 1] * feat.astype(F32)
            rhs[b * 128 : b * 128 + 128, :] = scaled.astype(BF16)
        dense = jnp.concatenate(
            [
                jnp.concatenate(
                    [tiles[slots[0, i * 32 + part * 8 + q]] for q in range(8)], axis=1
                )
                for i in range(8)
            ],
            axis=0,
        )
        term = jnp.dot(
            dense, rhs[part * 1024 : part * 1024 + 1024, :], preferred_element_type=F32
        )
        if part == 0:
            acc[...] = term
        elif part < 3:
            acc[...] += term
        else:
            total = (acc[...] + term).astype(BF16)
    for i in range(8):
        out[i, 0:128, :] = total[i * 128 : i * 128 + 128, :]
        out[i, 128:144, :] = sums[i]


def product(slots, recv_a, recv_b, tiles, sums):
    vmem = pl.BlockSpec(memory_space=pltpu.VMEM)
    return pl.pallas_call(
        product_kernel,
        in_specs=[pl.BlockSpec(memory_space=pltpu.SMEM), vmem, vmem, vmem, vmem],
        out_specs=vmem,
        scratch_shapes=[pltpu.VMEM((4096, 128), BF16), pltpu.VMEM((1024, 128), F32)],
        out_shape=jax.ShapeDtypeStruct((8, 144, 128), BF16),
        compiler_params=pltpu.CompilerParams(vmem_limit_bytes=24 << 20),
        name="product",
    )(slots, recv_a, recv_b, tiles, sums)


def node_kernel(parts, weight, bias, cotangent, hidden_ref, terms_ref):
    total = jnp.sum(parts[...].astype(F32), axis=0)
    row_degree = jnp.broadcast_to(1.0 + total[128:129, :] + total[136:137, :], (128, 128)).T
    aggregated = (lax.rsqrt(row_degree) * total[0:128, :]).astype(BF16)
    preact = jnp.dot(aggregated, weight[...], preferred_element_type=F32) + bias[...]
    logistic = jax.nn.sigmoid(preact)
    hidden_ref[...] = (preact * logistic).astype(BF16)
    grad = (
        cotangent[...].astype(F32) * logistic * (1.0 + preact * (1.0 - logistic))
    ).astype(BF16)
    weight_part = lax.dot_general(
        aggregated, grad, (((0,), (0,)), ((), ())), preferred_element_type=F32
    )
    bias_part = jnp.sum(grad.astype(F32), axis=0, keepdims=True)
    for k in range(32):
        half, f = k // 16, (k % 16) * 8
        for s in range(8):
            terms_ref[k, s, :, :] = weight_part[f + s : f + s + 1, half * 128 : half * 128 + 128]
        terms_ref[k, 8, :, :] = (
            bias_part[:, k * 128 : k * 128 + 128] if k < 2 else jnp.zeros((1, 128), F32)
        )


def nodes(parts, weight, bias, cotangent):
    return pl.pallas_call(
        node_kernel,
        out_shape=[
            jax.ShapeDtypeStruct((128, 256), BF16),
            jax.ShapeDtypeStruct((32, 9, 1, 128), F32),
        ],
        compiler_params=pltpu.CompilerParams(vmem_limit_bytes=16 << 20),
        name="nodes",
    )(parts, weight, bias, cotangent)


def finish_kernel(every, weight_ref, bias_ref):
    for k in range(32):
        half, f = k // 16, (k % 16) * 8
        for s in range(8):
            weight_ref[f + s : f + s + 1, half * 128 : half * 128 + 128] = every[k, s, :, :]
    for k in range(2):
        bias_ref[:, k * 128 : k * 128 + 128] = every[k, 8, :, :]


def finish(every):
    return pl.pallas_call(
        finish_kernel,
        out_shape=[
            jax.ShapeDtypeStruct((128, 256), F32),
            jax.ShapeDtypeStruct((1, 256), F32),
        ],
        compiler_params=pltpu.CompilerParams(vmem_limit_bytes=16 << 20),
        name="finish",
    )(every)


def gather(x, axes, count):
    return lax.all_to_all(jnp.broadcast_to(x[None], (count,) + x.shape), axes, 0, 0)


def body(features, weight, bias, cotangent, tile_values, tile_pos, tile_count, block_perm):
    packed = tile_values[0, 0]
    in_hbm = [
        pltpu.with_memory_space_constraint(x, pltpu.HBM)
        for x in (block_perm, tile_pos[0, 0], features, packed)
    ]
    send, slots, held = degrees(tile_count, *in_hbm)
    recv_a = lax.all_to_all(send, SAME_CORE_ROW, 0, 0)
    recv_b = lax.ppermute(recv_a, "core", SWAP)
    partial = product(slots, recv_a, recv_b, held, row_sums(slots, held))
    received = lax.all_to_all(partial, COL, 0, 0)
    hidden, terms = nodes(received, weight, bias[None], cotangent)
    own_terms = jnp.sum(lax.all_to_all(terms, PLANE, 0, 0), axis=0)
    total = jnp.sum(gather(own_terms, ("z",), 8), axis=0) * lax.rsqrt(F32(32768.0))
    weight_grad, bias_grad = finish(gather(total, PLANE, 32))
    return hidden, weight_grad, bias_grad[0]


def solution(mesh):
    split = Mesh(mesh.devices.reshape(8, 2, 2, 2, 4), ("z", "y_lo", "core", "y_hi", "x"))
    placed = (
        P(COL + ROW, None),
        P(),
        P(),
        P(ROW + COL, None),
        P(ROW, COL, None, None, None),
        P(ROW, COL, None, None),
        P(ROW, COL),
        P(),
    )
    return jax.shard_map(
        body,
        mesh=split,
        in_specs=placed,
        out_specs=(P(ROW + COL, None), P(), P()),
        check_vma=False,
    )
```

```python
import functools

import jax
import jax.numpy as jnp
from jax import lax
from jax.experimental import pallas as pl
from jax.experimental.pallas import tpu as pltpu
from jax.sharding import Mesh, PartitionSpec as P

ROW = ("z", "y_lo", "core")
COL = ("y_hi", "x")
SAME_CORE_ROW = ("z", "y_lo")
NEAR = ("y_lo", "core", "x")
FAR = ("z", "y_hi")
SWAP = [(0, 1), (1, 0)]
CHUNK = 16
F32 = jnp.float32
BF16 = jnp.bfloat16


def degree_kernel(
    count, perm_hbm, pos_hbm, feats_hbm, tiles_hbm, send_ref, slot_ref, tiles,
    perm, pos, feats, sums, sem, small,
):
    steps = 256 // CHUNK

    def chunk_copy(step):
        part = pl.ds(step * CHUNK, CHUNK)
        return pltpu.make_async_copy(tiles_hbm.at[part], tiles.at[part], sem.at[step])

    perm_copy = pltpu.make_async_copy(perm_hbm, perm, small.at[0])
    pos_copy = pltpu.make_async_copy(pos_hbm, pos, small.at[1])
    feats_copy = pltpu.make_async_copy(feats_hbm, feats, small.at[2])
    pos_copy.start()
    perm_copy.start()
    live_count = count[0, 0]

    @pl.loop(0, steps)
    def _(step):
        @pl.when(step * CHUNK < live_count)
        def _():
            chunk_copy(step).start()

    feats_copy.start()
    tiles[256] = jnp.zeros((128, 128), BF16)
    row, col, core = lax.axis_index(ROW), lax.axis_index(COL), lax.axis_index("core")
    perm_copy.wait()
    pos_copy.wait()
    own_row = jnp.zeros((1, 256), jnp.int32)
    own_col = jnp.zeros((1, 256), jnp.int32)
    for v in range(8):
        own_row += jnp.where(pos[0:1, :] == v, perm[row * 8 + v] - row * 8, 0)
    for v in range(32):
        own_col += jnp.where(pos[1:2, :] == v, perm[col * 32 + v] - col * 32, 0)
    place = (own_col >> 1) + 16 * ((own_col & 1) ^ core)
    slot = lax.broadcasted_iota(jnp.int32, (1, 256), 1)
    place = jnp.where(slot < live_count, place, 512)
    dense = own_row * 32 + place
    match = lax.broadcasted_iota(jnp.int32, (256, 256), 0) == dense
    number = lax.broadcasted_iota(jnp.int32, (16, 256), 1) + 1
    found = lax.dot_general(
        number.astype(F32).astype(BF16),
        match.astype(F32).astype(BF16),
        (((1,), (1,)), ((), ())),
        preferred_element_type=F32,
    )
    found = found[0:1, :].astype(jnp.int32)
    slot_ref[...] = jnp.where(found == 0, 256, found - 1)

    @pl.loop(0, steps)
    def _(step):
        base = step * CHUNK

        @pl.when(base < live_count)
        def _():
            chunk_copy(step).wait()
            for group in range(CHUNK // 8):
                rows = []
                for u in range(8):
                    tile = tiles[base + group * 8 + u].astype(F32)
                    rows.append(jnp.sum(tile, axis=0, keepdims=True))
                sums[pl.ds(base + group * 8, 8), :] = jnp.concatenate(rows, axis=0)

        @pl.when(base >= live_count)
        def _():
            sums[pl.ds(base, CHUNK), :] = jnp.zeros((CHUNK, 128), F32)

    pick = (lax.broadcasted_iota(jnp.int32, (32, 256), 0) == place).astype(F32).astype(BF16)
    high = sums[...].astype(BF16)
    low = (sums[...] - high.astype(F32)).astype(BF16)
    col_part = jnp.dot(pick, high, preferred_element_type=F32)
    col_part += jnp.dot(pick, low, preferred_element_type=F32)
    feats_copy.wait()
    for m in range(16):
        send_ref[m, 0:128, :] = feats[...]
        send_ref[m, 128:160, :] = col_part.astype(BF16)


def degrees(*arrays):
    vmem = pl.BlockSpec(memory_space=pltpu.VMEM)
    hbm = pl.BlockSpec(memory_space=pltpu.HBM)
    return pl.pallas_call(
        degree_kernel,
        in_specs=[pl.BlockSpec(memory_space=pltpu.SMEM)] + [hbm] * 4,
        out_specs=[vmem, vmem, vmem],
        scratch_shapes=[
            pltpu.SMEM((256,), jnp.int32),
            pltpu.VMEM((2, 256), jnp.int32),
            pltpu.VMEM((128, 128), BF16),
            pltpu.VMEM((256, 128), F32),
            pltpu.SemaphoreType.DMA((256 // CHUNK,)),
            pltpu.SemaphoreType.DMA((3,)),
        ],
        out_shape=[
            jax.ShapeDtypeStruct((16, 160, 128), BF16),
            jax.ShapeDtypeStruct((1, 256), jnp.int32),
            pltpu.VMEM((257, 128, 128), BF16),
        ],
        compiler_params=pltpu.CompilerParams(vmem_limit_bytes=16 << 20),
        name="degrees",
    )(*arrays)


def row_sum_kernel(slots, tiles, sums_ref):
    @pl.loop(0, 8)
    def _(i):
        total = jnp.zeros((128, 128), F32)
        for place in range(32):
            total += tiles[slots[0, i * 32 + place]].astype(F32)
        sums = jnp.broadcast_to(jnp.sum(total.T, axis=0, keepdims=True), (8, 128))
        high = sums.astype(BF16)
        low = (sums - high.astype(F32)).astype(BF16)
        sums_ref[i] = jnp.concatenate([high, low], axis=0)


def row_sums(slots, tiles):
    vmem = pl.BlockSpec(memory_space=pltpu.VMEM)
    return pl.pallas_call(
        row_sum_kernel,
        in_specs=[pl.BlockSpec(memory_space=pltpu.SMEM), vmem],
        out_specs=vmem,
        out_shape=pltpu.VMEM((8, 16, 128), BF16),
        cost_estimate=pl.CostEstimate(flops=0, bytes_accessed=6 << 20, transcendentals=0),
        compiler_params=pltpu.CompilerParams(vmem_limit_bytes=16 << 20),
        name="row_sums",
    )(slots, tiles)


def product_kernel(slots, recv_a, recv_b, tiles, sums, out, rhs, acc):
    from_a = jnp.sum(recv_a[:, 128:160, :].astype(F32), axis=0)
    from_b = jnp.sum(recv_b[:, 128:160, :].astype(F32), axis=0)
    degree = 1.0 + from_a + jnp.concatenate([from_b[16:32], from_b[0:16]], axis=0)
    scale = jnp.concatenate([lax.rsqrt(degree), jnp.zeros((96, 128), F32)], axis=0).T
    for part in range(4):
        for b in range(part * 8, part * 8 + 8):
            feat = recv_a[b, 0:128, :] if b < 16 else recv_b[b - 16, 0:128, :]
            scaled = scale[:, b : b + 1] * feat.astype(F32)
            rhs[b * 128 : b * 128 + 128, :] = scaled.astype(BF16)
        dense = jnp.concatenate(
            [
                jnp.concatenate(
                    [tiles[slots[0, i * 32 + part * 8 + q]] for q in range(8)], axis=1
                )
                for i in range(8)
            ],
            axis=0,
        )
        term = jnp.dot(
            dense, rhs[part * 1024 : part * 1024 + 1024, :], preferred_element_type=F32
        )
        if part == 0:
            acc[...] = term
        elif part < 3:
            acc[...] += term
        else:
            total = (acc[...] + term).astype(BF16)
    for i in range(8):
        out[i, 0:128, :] = total[i * 128 : i * 128 + 128, :]
        out[i, 128:144, :] = sums[i]


def product(slots, recv_a, recv_b, tiles, sums):
    vmem = pl.BlockSpec(memory_space=pltpu.VMEM)
    return pl.pallas_call(
        product_kernel,
        in_specs=[pl.BlockSpec(memory_space=pltpu.SMEM), vmem, vmem, vmem, vmem],
        out_specs=vmem,
        scratch_shapes=[pltpu.VMEM((4096, 128), BF16), pltpu.VMEM((1024, 128), F32)],
        out_shape=jax.ShapeDtypeStruct((8, 144, 128), BF16),
        compiler_params=pltpu.CompilerParams(vmem_limit_bytes=24 << 20),
        name="product",
    )(slots, recv_a, recv_b, tiles, sums)


def node_kernel(parts, weight, bias, cotangent, hidden_ref, terms_ref):
    total = jnp.sum(parts[...].astype(F32), axis=0)
    row_degree = jnp.broadcast_to(1.0 + total[128:129, :] + total[136:137, :], (128, 128)).T
    aggregated = (lax.rsqrt(row_degree) * total[0:128, :]).astype(BF16)
    preact = jnp.dot(aggregated, weight[...], preferred_element_type=F32) + bias[...]
    logistic = jax.nn.sigmoid(preact)
    hidden_ref[...] = (preact * logistic).astype(BF16)
    grad = (
        cotangent[...].astype(F32) * logistic * (1.0 + preact * (1.0 - logistic))
    ).astype(BF16)
    weight_part = lax.dot_general(
        aggregated, grad, (((0,), (0,)), ((), ())), preferred_element_type=F32
    )
    bias_part = jnp.sum(grad.astype(F32), axis=0, keepdims=True)
    for k in range(16):
        for half in range(2):
            for f in range(8):
                terms_ref[k, half * 8 + f, :, :] = weight_part[
                    k * 8 + f : k * 8 + f + 1, half * 128 : half * 128 + 128
                ]
        terms_ref[k, 16, :, :] = (
            bias_part[:, k * 128 : k * 128 + 128] if k < 2 else jnp.zeros((1, 128), F32)
        )


def nodes(parts, weight, bias, cotangent):
    return pl.pallas_call(
        node_kernel,
        out_shape=[
            jax.ShapeDtypeStruct((128, 256), BF16),
            jax.ShapeDtypeStruct((16, 17, 1, 128), F32),
        ],
        compiler_params=pltpu.CompilerParams(vmem_limit_bytes=16 << 20),
        name="nodes",
    )(parts, weight, bias, cotangent)


def finish_kernel(every, weight_ref, bias_ref):
    for k in range(16):
        for half in range(2):
            for f in range(8):
                weight_ref[k * 8 + f : k * 8 + f + 1, half * 128 : half * 128 + 128] = every[
                    k, half * 8 + f, :, :
                ]
    for k in range(2):
        bias_ref[:, k * 128 : k * 128 + 128] = every[k, 16, :, :]


def finish(every):
    return pl.pallas_call(
        finish_kernel,
        out_shape=[
            jax.ShapeDtypeStruct((128, 256), F32),
            jax.ShapeDtypeStruct((1, 256), F32),
        ],
        compiler_params=pltpu.CompilerParams(vmem_limit_bytes=16 << 20),
        name="finish",
    )(every)


def gather(x, axes, count):
    return lax.all_to_all(jnp.broadcast_to(x[None], (count,) + x.shape), axes, 0, 0)


def body(features, weight, bias, cotangent, tile_values, tile_pos, tile_count, block_perm):
    packed = tile_values[0, 0]
    in_hbm = [
        pltpu.with_memory_space_constraint(x, pltpu.HBM)
        for x in (block_perm, tile_pos[0, 0], features, packed)
    ]
    send, slots, held = degrees(tile_count, *in_hbm)
    recv_a = lax.all_to_all(send, SAME_CORE_ROW, 0, 0)
    recv_b = lax.ppermute(recv_a, "core", SWAP)
    partial = product(slots, recv_a, recv_b, held, row_sums(slots, held))
    received = lax.all_to_all(partial, COL, 0, 0)
    hidden, terms = nodes(received, weight, bias[None], cotangent)
    own_terms = jnp.sum(lax.all_to_all(terms, NEAR, 0, 0), axis=0)
    total = jnp.sum(gather(own_terms, FAR, 16), axis=0) * lax.rsqrt(F32(32768.0))
    weight_grad, bias_grad = finish(gather(total, NEAR, 16))
    return hidden, weight_grad, bias_grad[0]


def solution(mesh):
    split = Mesh(mesh.devices.reshape(8, 2, 2, 2, 4), ("z", "y_lo", "core", "y_hi", "x"))
    placed = (
        P(COL + ROW, None),
        P(),
        P(),
        P(ROW + COL, None),
        P(ROW, COL, None, None, None),
        P(ROW, COL, None, None),
        P(ROW, COL),
        P(),
    )
    return jax.shard_map(
        body,
        mesh=split,
        in_specs=placed,
        out_specs=(P(ROW + COL, None), P(), P()),
        check_vma=False,
    )
```

```python
import functools

import jax
import jax.numpy as jnp
from jax import lax
from jax.experimental import pallas as pl
from jax.experimental.pallas import tpu as pltpu
from jax.sharding import Mesh, PartitionSpec as P

ROW = ("z", "y_lo", "core")
COL = ("y_hi", "x")
SAME_CORE_ROW = ("z", "y_lo")
NEAR = ("y_lo", "core", "x")
FAR = ("z", "y_hi")
SWAP = [(0, 1), (1, 0)]
CHUNK = 16
F32 = jnp.float32
BF16 = jnp.bfloat16


def degree_kernel(
    count, perm_hbm, pos_hbm, feats_hbm, tiles_hbm, send_ref, slot_ref, tiles,
    perm, pos, feats, sums, sem, small,
):
    steps = 256 // CHUNK

    def chunk_copy(step):
        part = pl.ds(step * CHUNK, CHUNK)
        return pltpu.make_async_copy(tiles_hbm.at[part], tiles.at[part], sem.at[step])

    perm_copy = pltpu.make_async_copy(perm_hbm, perm, small.at[0])
    pos_copy = pltpu.make_async_copy(pos_hbm, pos, small.at[1])
    feats_copy = pltpu.make_async_copy(feats_hbm, feats, small.at[2])
    pos_copy.start()
    perm_copy.start()
    live_count = count[0, 0]

    @pl.loop(0, steps)
    def _(step):
        @pl.when(step * CHUNK < live_count)
        def _():
            chunk_copy(step).start()

    feats_copy.start()
    tiles[256] = jnp.zeros((128, 128), BF16)
    row, col, core = lax.axis_index(ROW), lax.axis_index(COL), lax.axis_index("core")
    perm_copy.wait()
    pos_copy.wait()
    own_row = jnp.zeros((1, 256), jnp.int32)
    own_col = jnp.zeros((1, 256), jnp.int32)
    for v in range(8):
        own_row += jnp.where(pos[0:1, :] == v, perm[row * 8 + v] - row * 8, 0)
    for v in range(32):
        own_col += jnp.where(pos[1:2, :] == v, perm[col * 32 + v] - col * 32, 0)
    place = (own_col >> 1) + 16 * ((own_col & 1) ^ core)
    slot = lax.broadcasted_iota(jnp.int32, (1, 256), 1)
    place = jnp.where(slot < live_count, place, 512)
    dense = own_row * 32 + place
    match = lax.broadcasted_iota(jnp.int32, (256, 256), 0) == dense
    number = lax.broadcasted_iota(jnp.int32, (16, 256), 1) + 1
    found = lax.dot_general(
        number.astype(F32).astype(BF16),
        match.astype(F32).astype(BF16),
        (((1,), (1,)), ((), ())),
        preferred_element_type=F32,
    )
    found = found[0:1, :].astype(jnp.int32)
    slot_ref[...] = jnp.where(found == 0, 256, found - 1)

    @pl.loop(0, steps)
    def _(step):
        base = step * CHUNK

        @pl.when(base < live_count)
        def _():
            chunk_copy(step).wait()
            for group in range(CHUNK // 8):
                rows = []
                for u in range(8):
                    tile = tiles[base + group * 8 + u].astype(F32)
                    rows.append(jnp.sum(tile, axis=0, keepdims=True))
                sums[pl.ds(base + group * 8, 8), :] = jnp.concatenate(rows, axis=0)

        @pl.when(base >= live_count)
        def _():
            sums[pl.ds(base, CHUNK), :] = jnp.zeros((CHUNK, 128), F32)

    pick = (lax.broadcasted_iota(jnp.int32, (32, 256), 0) == place).astype(F32).astype(BF16)
    high = sums[...].astype(BF16)
    low = (sums[...] - high.astype(F32)).astype(BF16)
    col_part = jnp.dot(pick, high, preferred_element_type=F32)
    col_part += jnp.dot(pick, low, preferred_element_type=F32)
    feats_copy.wait()
    for m in range(16):
        send_ref[m, 0:128, :] = feats[...]
        send_ref[m, 128:160, :] = col_part.astype(BF16)


def degrees(*arrays):
    vmem = pl.BlockSpec(memory_space=pltpu.VMEM)
    hbm = pl.BlockSpec(memory_space=pltpu.HBM)
    return pl.pallas_call(
        degree_kernel,
        in_specs=[pl.BlockSpec(memory_space=pltpu.SMEM)] + [hbm] * 4,
        out_specs=[vmem, vmem, vmem],
        scratch_shapes=[
            pltpu.SMEM((256,), jnp.int32),
            pltpu.VMEM((2, 256), jnp.int32),
            pltpu.VMEM((128, 128), BF16),
            pltpu.VMEM((256, 128), F32),
            pltpu.SemaphoreType.DMA((256 // CHUNK,)),
            pltpu.SemaphoreType.DMA((3,)),
        ],
        out_shape=[
            jax.ShapeDtypeStruct((16, 160, 128), BF16),
            jax.ShapeDtypeStruct((1, 256), jnp.int32),
            pltpu.VMEM((257, 128, 128), BF16),
        ],
        compiler_params=pltpu.CompilerParams(vmem_limit_bytes=16 << 20),
        name="degrees",
    )(*arrays)


def row_sum_kernel(slots, tiles, sums_ref):
    for i in range(8):
        total = jnp.zeros((128, 128), F32)
        for place in range(0, 32, 2):
            one, two = slots[0, i * 32 + place], slots[0, i * 32 + place + 1]
            total += (tiles[one] + tiles[two]).astype(F32)
        sums = jnp.broadcast_to(jnp.sum(total.T, axis=0, keepdims=True), (8, 128))
        high = sums.astype(BF16)
        low = (sums - high.astype(F32)).astype(BF16)
        sums_ref[i] = jnp.concatenate([high, low], axis=0)


def row_sums(slots, tiles):
    vmem = pl.BlockSpec(memory_space=pltpu.VMEM)
    return pl.pallas_call(
        row_sum_kernel,
        in_specs=[pl.BlockSpec(memory_space=pltpu.SMEM), vmem],
        out_specs=vmem,
        out_shape=pltpu.VMEM((8, 16, 128), BF16),
        cost_estimate=pl.CostEstimate(flops=0, bytes_accessed=3 << 20, transcendentals=0),
        compiler_params=pltpu.CompilerParams(vmem_limit_bytes=16 << 20),
        name="row_sums",
    )(slots, tiles)


def cell_part(slots, tiles, recv, scale, rhs, first):
    terms = []
    for part in range(2):
        for b in range(part * 8, part * 8 + 8):
            scaled = scale[:, first + b : first + b + 1] * recv[b, 0:128, :].astype(F32)
            rhs[b * 128 : b * 128 + 128, :] = scaled.astype(BF16)
        dense = jnp.concatenate(
            [
                jnp.concatenate(
                    [tiles[slots[0, i * 32 + first + part * 8 + q]] for q in range(8)], axis=1
                )
                for i in range(8)
            ],
            axis=0,
        )
        block = rhs[part * 1024 : part * 1024 + 1024, :]
        terms.append(jnp.dot(dense, block, preferred_element_type=F32))
    return terms


def near_kernel(slots, deg_a, deg_b, recv, tiles, acc, scale_ref, rhs):
    from_b = deg_b[...]
    degree = 1.0 + deg_a[...] + jnp.concatenate([from_b[16:32], from_b[0:16]], axis=0)
    scale = jnp.concatenate([lax.rsqrt(degree), jnp.zeros((96, 128), F32)], axis=0).T
    scale_ref[...] = scale
    first, second = cell_part(slots, tiles, recv, scale, rhs, 0)
    acc[...] = first
    acc[...] += second


def near_product(*arrays):
    vmem = pl.BlockSpec(memory_space=pltpu.VMEM)
    return pl.pallas_call(
        near_kernel,
        in_specs=[pl.BlockSpec(memory_space=pltpu.SMEM)] + [vmem] * 4,
        out_specs=[vmem, vmem],
        scratch_shapes=[pltpu.VMEM((2048, 128), BF16)],
        out_shape=[pltpu.VMEM((1024, 128), F32), pltpu.VMEM((128, 128), F32)],
        cost_estimate=pl.CostEstimate(flops=1 << 29, bytes_accessed=5 << 20, transcendentals=0),
        compiler_params=pltpu.CompilerParams(vmem_limit_bytes=16 << 20),
        name="near_product",
    )(*arrays)


def far_kernel(slots, recv, scale, acc, tiles, sums, out, rhs, half):
    first, second = cell_part(slots, tiles, recv, scale, rhs, 16)
    half[...] = acc[...] + first
    total = (half[...] + second).astype(BF16)
    for i in range(8):
        out[i, 0:128, :] = total[i * 128 : i * 128 + 128, :]
        out[i, 128:144, :] = sums[i]


def far_product(*arrays):
    vmem = pl.BlockSpec(memory_space=pltpu.VMEM)
    return pl.pallas_call(
        far_kernel,
        in_specs=[pl.BlockSpec(memory_space=pltpu.SMEM)] + [vmem] * 5,
        out_specs=vmem,
        scratch_shapes=[pltpu.VMEM((2048, 128), BF16), pltpu.VMEM((1024, 128), F32)],
        out_shape=jax.ShapeDtypeStruct((8, 144, 128), BF16),
        compiler_params=pltpu.CompilerParams(vmem_limit_bytes=16 << 20),
        name="far_product",
    )(*arrays)


def node_kernel(parts, weight, bias, cotangent, hidden_ref, terms_ref):
    total = jnp.sum(parts[...].astype(F32), axis=0)
    row_degree = jnp.broadcast_to(1.0 + total[128:129, :] + total[136:137, :], (128, 128)).T
    aggregated = (lax.rsqrt(row_degree) * total[0:128, :]).astype(BF16)
    preact = jnp.dot(aggregated, weight[...], preferred_element_type=F32) + bias[...]
    logistic = jax.nn.sigmoid(preact)
    hidden_ref[...] = (preact * logistic).astype(BF16)
    grad = (
        cotangent[...].astype(F32) * logistic * (1.0 + preact * (1.0 - logistic))
    ).astype(BF16)
    weight_part = lax.dot_general(
        aggregated, grad, (((0,), (0,)), ((), ())), preferred_element_type=F32
    )
    bias_part = jnp.sum(grad.astype(F32), axis=0, keepdims=True)
    for k in range(16):
        for half in range(2):
            for f in range(8):
                terms_ref[k, half * 8 + f, :, :] = weight_part[
                    k * 8 + f : k * 8 + f + 1, half * 128 : half * 128 + 128
                ]
        terms_ref[k, 16, :, :] = (
            bias_part[:, k * 128 : k * 128 + 128] if k < 2 else jnp.zeros((1, 128), F32)
        )


def nodes(parts, weight, bias, cotangent):
    return pl.pallas_call(
        node_kernel,
        out_shape=[
            jax.ShapeDtypeStruct((128, 256), BF16),
            jax.ShapeDtypeStruct((16, 17, 1, 128), F32),
        ],
        compiler_params=pltpu.CompilerParams(vmem_limit_bytes=16 << 20),
        name="nodes",
    )(parts, weight, bias, cotangent)


def finish_kernel(every, weight_ref, bias_ref):
    for k in range(16):
        for half in range(2):
            for f in range(8):
                weight_ref[k * 8 + f : k * 8 + f + 1, half * 128 : half * 128 + 128] = every[
                    k, half * 8 + f, :, :
                ]
    for k in range(2):
        bias_ref[:, k * 128 : k * 128 + 128] = every[k, 16, :, :]


def finish(every):
    return pl.pallas_call(
        finish_kernel,
        out_shape=[
            jax.ShapeDtypeStruct((128, 256), F32),
            jax.ShapeDtypeStruct((1, 256), F32),
        ],
        compiler_params=pltpu.CompilerParams(vmem_limit_bytes=16 << 20),
        name="finish",
    )(every)


def gather(x, axes, count):
    return lax.all_to_all(jnp.broadcast_to(x[None], (count,) + x.shape), axes, 0, 0)


def body(features, weight, bias, cotangent, tile_values, tile_pos, tile_count, block_perm):
    packed = tile_values[0, 0]
    in_hbm = [
        pltpu.with_memory_space_constraint(x, pltpu.HBM)
        for x in (block_perm, tile_pos[0, 0], features, packed)
    ]
    send, slots, held = degrees(tile_count, *in_hbm)
    recv_a = lax.all_to_all(send, SAME_CORE_ROW, 0, 0)
    deg_a = jnp.sum(recv_a[:, 128:160, :].astype(F32), axis=0)
    deg_b = lax.ppermute(deg_a, "core", SWAP)
    recv_b = lax.ppermute(recv_a, "core", SWAP)
    acc, scale = near_product(slots, deg_a, deg_b, recv_a, held)
    partial = far_product(slots, recv_b, scale, acc, held, row_sums(slots, held))
    received = lax.all_to_all(partial, COL, 0, 0)
    hidden, terms = nodes(received, weight, bias[None], cotangent)
    own_terms = jnp.sum(lax.all_to_all(terms, NEAR, 0, 0), axis=0)
    total = jnp.sum(gather(own_terms, FAR, 16), axis=0) * lax.rsqrt(F32(32768.0))
    weight_grad, bias_grad = finish(gather(total, NEAR, 16))
    return hidden, weight_grad, bias_grad[0]


def solution(mesh):
    split = Mesh(mesh.devices.reshape(8, 2, 2, 2, 4), ("z", "y_lo", "core", "y_hi", "x"))
    placed = (
        P(COL + ROW, None),
        P(),
        P(),
        P(ROW + COL, None),
        P(ROW, COL, None, None, None),
        P(ROW, COL, None, None),
        P(ROW, COL),
        P(),
    )
    return jax.shard_map(
        body,
        mesh=split,
        in_specs=placed,
        out_specs=(P(ROW + COL, None), P(), P()),
        check_vma=False,
    )
```

```python
import functools

import jax
import jax.numpy as jnp
from jax import lax
from jax.experimental import pallas as pl
from jax.experimental.pallas import tpu as pltpu
from jax.sharding import Mesh, PartitionSpec as P

ROW = ("z", "y_lo", "core")
COL = ("y_hi", "x")
SAME_CORE_ROW = ("z", "y_lo")
NEAR = ("y_lo", "core", "x")
FAR = ("z", "y_hi")
SWAP = [(0, 1), (1, 0)]
CHUNK = 16
F32 = jnp.float32
BF16 = jnp.bfloat16


def degree_kernel(
    count, perm_hbm, pos_hbm, feats_hbm, tiles_hbm, send_ref, slot_ref, tiles,
    perm, pos, feats, sums, places, sem, small,
):
    steps = 256 // CHUNK

    def chunk_copy(step):
        part = pl.ds(step * CHUNK, CHUNK)
        return pltpu.make_async_copy(tiles_hbm.at[part], tiles.at[part], sem.at[step])

    perm_copy = pltpu.make_async_copy(perm_hbm, perm, small.at[0])
    pos_copy = pltpu.make_async_copy(pos_hbm, pos, small.at[1])
    feats_copy = pltpu.make_async_copy(feats_hbm, feats, small.at[2])
    pos_copy.start()
    perm_copy.start()
    live_count = count[0, 0]

    @pl.loop(0, steps)
    def _(step):
        @pl.when(step * CHUNK < live_count)
        def _():
            chunk_copy(step).start()

    feats_copy.start()
    tiles[256] = jnp.zeros((128, 128), BF16)
    row, col, core = lax.axis_index(ROW), lax.axis_index(COL), lax.axis_index("core")
    perm_copy.wait()
    pos_copy.wait()
    own_row = jnp.zeros((1, 256), jnp.int32)
    own_col = jnp.zeros((1, 256), jnp.int32)
    for v in range(8):
        own_row += jnp.where(pos[0:1, :] == v, perm[row * 8 + v] - row * 8, 0)
    for v in range(32):
        own_col += jnp.where(pos[1:2, :] == v, perm[col * 32 + v] - col * 32, 0)
    place = (own_col >> 1) + 16 * ((own_col & 1) ^ core)
    slot = lax.broadcasted_iota(jnp.int32, (1, 256), 1)
    place = jnp.where(slot < live_count, place, 512)
    dense = own_row * 32 + place
    match = lax.broadcasted_iota(jnp.int32, (256, 256), 0) == dense
    number = lax.broadcasted_iota(jnp.int32, (16, 256), 1) + 1
    found = lax.dot_general(
        number.astype(F32).astype(BF16),
        match.astype(F32).astype(BF16),
        (((1,), (1,)), ((), ())),
        preferred_element_type=F32,
    )
    found = found[0:1, :].astype(jnp.int32)
    places[...] = jnp.where(found == 0, 256, found - 1)
    slot_copy = pltpu.make_async_copy(places, slot_ref, small.at[3])
    slot_copy.start()

    @pl.loop(0, steps)
    def _(step):
        base = step * CHUNK

        @pl.when(base < live_count)
        def _():
            chunk_copy(step).wait()
            for group in range(CHUNK // 8):
                rows = []
                for u in range(8):
                    tile = tiles[base + group * 8 + u].astype(F32)
                    rows.append(jnp.sum(tile, axis=0, keepdims=True))
                sums[pl.ds(base + group * 8, 8), :] = jnp.concatenate(rows, axis=0)

        @pl.when(base >= live_count)
        def _():
            sums[pl.ds(base, CHUNK), :] = jnp.zeros((CHUNK, 128), F32)

    pick = (lax.broadcasted_iota(jnp.int32, (32, 256), 0) == place).astype(F32).astype(BF16)
    high = sums[...].astype(BF16)
    low = (sums[...] - high.astype(F32)).astype(BF16)
    col_part = jnp.dot(pick, high, preferred_element_type=F32)
    col_part += jnp.dot(pick, low, preferred_element_type=F32)
    slot_copy.wait()
    feats_copy.wait()
    for m in range(16):
        send_ref[m, 0:128, :] = feats[...]
        send_ref[m, 128:160, :] = col_part.astype(BF16)


def degrees(*arrays):
    vmem = pl.BlockSpec(memory_space=pltpu.VMEM)
    hbm = pl.BlockSpec(memory_space=pltpu.HBM)
    return pl.pallas_call(
        degree_kernel,
        in_specs=[pl.BlockSpec(memory_space=pltpu.SMEM)] + [hbm] * 4,
        out_specs=[vmem, pl.BlockSpec(memory_space=pltpu.SMEM), vmem],
        scratch_shapes=[
            pltpu.SMEM((256,), jnp.int32),
            pltpu.VMEM((2, 256), jnp.int32),
            pltpu.VMEM((128, 128), BF16),
            pltpu.VMEM((256, 128), F32),
            pltpu.VMEM((1, 256), jnp.int32),
            pltpu.SemaphoreType.DMA((256 // CHUNK,)),
            pltpu.SemaphoreType.DMA((4,)),
        ],
        out_shape=[
            jax.ShapeDtypeStruct((16, 160, 128), BF16),
            pltpu.SMEM((1, 256), jnp.int32),
            pltpu.VMEM((257, 128, 128), BF16),
        ],
        compiler_params=pltpu.CompilerParams(vmem_limit_bytes=16 << 20),
        name="degrees",
    )(*arrays)


def row_sum_kernel(slots, tiles, sums_ref):
    ones = jnp.ones((16, 128), BF16)

    @pl.loop(0, 8)
    def _(i):
        total = jnp.zeros((128, 128), F32)
        for place in range(0, 32, 2):
            one, two = slots[0, i * 32 + place], slots[0, i * 32 + place + 1]
            total += (tiles[one] + tiles[two]).astype(F32)
        high = total.astype(BF16)
        low = (total - high.astype(F32)).astype(BF16)
        dims = (((1,), (1,)), ((), ()))
        sums = lax.dot_general(ones, high, dims, preferred_element_type=F32)
        sums += lax.dot_general(ones, low, dims, preferred_element_type=F32)
        high = sums.astype(BF16)
        low = (sums - high.astype(F32)).astype(BF16)
        sums_ref[i] = jnp.concatenate([high[0:8], low[0:8]], axis=0)


def row_sums(slots, tiles):
    vmem = pl.BlockSpec(memory_space=pltpu.VMEM)
    return pl.pallas_call(
        row_sum_kernel,
        in_specs=[pl.BlockSpec(memory_space=pltpu.SMEM), vmem],
        out_specs=vmem,
        out_shape=pltpu.VMEM((8, 16, 128), BF16),
        cost_estimate=pl.CostEstimate(flops=0, bytes_accessed=6 << 20, transcendentals=0),
        compiler_params=pltpu.CompilerParams(vmem_limit_bytes=16 << 20),
        name="row_sums",
    )(slots, tiles)


def product_kernel(slots, recv_a, recv_b, tiles, sums, out, rhs, acc):
    from_a = jnp.sum(recv_a[:, 128:160, :].astype(F32), axis=0)
    from_b = jnp.sum(recv_b[:, 128:160, :].astype(F32), axis=0)
    degree = 1.0 + from_a + jnp.concatenate([from_b[16:32], from_b[0:16]], axis=0)
    scale = jnp.concatenate([lax.rsqrt(degree), jnp.zeros((96, 128), F32)], axis=0).T
    for part in range(4):
        for b in range(part * 8, part * 8 + 8):
            feat = recv_a[b, 0:128, :] if b < 16 else recv_b[b - 16, 0:128, :]
            scaled = scale[:, b : b + 1] * feat.astype(F32)
            rhs[b * 128 : b * 128 + 128, :] = scaled.astype(BF16)
        dense = jnp.concatenate(
            [
                jnp.concatenate(
                    [tiles[slots[0, i * 32 + part * 8 + q]] for q in range(8)], axis=1
                )
                for i in range(8)
            ],
            axis=0,
        )
        term = jnp.dot(
            dense, rhs[part * 1024 : part * 1024 + 1024, :], preferred_element_type=F32
        )
        if part == 0:
            acc[...] = term
        elif part < 3:
            acc[...] += term
        else:
            total = (acc[...] + term).astype(BF16)
    for i in range(8):
        out[i, 0:128, :] = total[i * 128 : i * 128 + 128, :]
        out[i, 128:144, :] = sums[i]


def product(slots, recv_a, recv_b, tiles, sums):
    vmem = pl.BlockSpec(memory_space=pltpu.VMEM)
    return pl.pallas_call(
        product_kernel,
        in_specs=[pl.BlockSpec(memory_space=pltpu.SMEM), vmem, vmem, vmem, vmem],
        out_specs=vmem,
        scratch_shapes=[pltpu.VMEM((4096, 128), BF16), pltpu.VMEM((1024, 128), F32)],
        out_shape=jax.ShapeDtypeStruct((8, 144, 128), BF16),
        compiler_params=pltpu.CompilerParams(vmem_limit_bytes=24 << 20),
        name="product",
    )(slots, recv_a, recv_b, tiles, sums)


def node_kernel(parts, weight, bias, cotangent, hidden_ref, terms_ref):
    total = jnp.sum(parts[...].astype(F32), axis=0)
    row_degree = jnp.broadcast_to(1.0 + total[128:129, :] + total[136:137, :], (128, 128)).T
    aggregated = (lax.rsqrt(row_degree) * total[0:128, :]).astype(BF16)
    preact = jnp.dot(aggregated, weight[...], preferred_element_type=F32) + bias[...]
    logistic = jax.nn.sigmoid(preact)
    hidden_ref[...] = (preact * logistic).astype(BF16)
    grad = (
        cotangent[...].astype(F32) * logistic * (1.0 + preact * (1.0 - logistic))
    ).astype(BF16)
    weight_part = lax.dot_general(
        aggregated, grad, (((0,), (0,)), ((), ())), preferred_element_type=F32
    )
    bias_part = jnp.sum(grad.astype(F32), axis=0, keepdims=True)
    for k in range(16):
        for half in range(2):
            for f in range(8):
                terms_ref[k, half * 8 + f, :, :] = weight_part[
                    k * 8 + f : k * 8 + f + 1, half * 128 : half * 128 + 128
                ]
        terms_ref[k, 16, :, :] = (
            bias_part[:, k * 128 : k * 128 + 128] if k < 2 else jnp.zeros((1, 128), F32)
        )


def nodes(parts, weight, bias, cotangent):
    return pl.pallas_call(
        node_kernel,
        out_shape=[
            jax.ShapeDtypeStruct((128, 256), BF16),
            jax.ShapeDtypeStruct((16, 17, 1, 128), F32),
        ],
        compiler_params=pltpu.CompilerParams(vmem_limit_bytes=16 << 20),
        name="nodes",
    )(parts, weight, bias, cotangent)


def finish_kernel(every, weight_ref, bias_ref):
    for k in range(16):
        for half in range(2):
            for f in range(8):
                weight_ref[k * 8 + f : k * 8 + f + 1, half * 128 : half * 128 + 128] = every[
                    k, half * 8 + f, :, :
                ]
    for k in range(2):
        bias_ref[:, k * 128 : k * 128 + 128] = every[k, 16, :, :]


def finish(every):
    return pl.pallas_call(
        finish_kernel,
        out_shape=[
            jax.ShapeDtypeStruct((128, 256), F32),
            jax.ShapeDtypeStruct((1, 256), F32),
        ],
        compiler_params=pltpu.CompilerParams(vmem_limit_bytes=16 << 20),
        name="finish",
    )(every)


def gather(x, axes, count):
    return lax.all_to_all(jnp.broadcast_to(x[None], (count,) + x.shape), axes, 0, 0)


def body(features, weight, bias, cotangent, tile_values, tile_pos, tile_count, block_perm):
    packed = tile_values[0, 0]
    in_hbm = [
        pltpu.with_memory_space_constraint(x, pltpu.HBM)
        for x in (block_perm, tile_pos[0, 0], features, packed)
    ]
    send, slots, held = degrees(tile_count, *in_hbm)
    recv_a = lax.all_to_all(send, SAME_CORE_ROW, 0, 0)
    recv_b = lax.ppermute(recv_a, "core", SWAP)
    partial = product(slots, recv_a, recv_b, held, row_sums(slots, held))
    received = lax.all_to_all(partial, COL, 0, 0)
    hidden, terms = nodes(received, weight, bias[None], cotangent)
    own_terms = jnp.sum(lax.all_to_all(terms, NEAR, 0, 0), axis=0)
    total = jnp.sum(gather(own_terms, FAR, 16), axis=0) * lax.rsqrt(F32(32768.0))
    weight_grad, bias_grad = finish(gather(total, NEAR, 16))
    return hidden, weight_grad, bias_grad[0]


def solution(mesh):
    split = Mesh(mesh.devices.reshape(8, 2, 2, 2, 4), ("z", "y_lo", "core", "y_hi", "x"))
    placed = (
        P(COL + ROW, None),
        P(),
        P(),
        P(ROW + COL, None),
        P(ROW, COL, None, None, None),
        P(ROW, COL, None, None),
        P(ROW, COL),
        P(),
    )
    return jax.shard_map(
        body,
        mesh=split,
        in_specs=placed,
        out_specs=(P(ROW + COL, None), P(), P()),
        check_vma=False,
    )
```

```python
import functools

import jax
import jax.numpy as jnp
from jax import lax
from jax.experimental import pallas as pl
from jax.experimental.pallas import tpu as pltpu
from jax.sharding import Mesh, PartitionSpec as P

ROW = ("z", "y_lo", "core")
COL = ("y_hi", "x")
SAME_CORE_ROW = ("z", "y_lo")
NEAR = ("y_lo", "core", "x")
FAR = ("z", "y_hi")
SWAP = [(0, 1), (1, 0)]
CHUNK = 16
F32 = jnp.float32
BF16 = jnp.bfloat16


def degree_kernel(
    count, perm_hbm, pos_hbm, feats_hbm, tiles_hbm, send_ref, slot_ref, tiles,
    perm, pos, feats, sums, places, sem, small,
):
    steps = 256 // CHUNK

    def chunk_copy(step):
        part = pl.ds(step * CHUNK, CHUNK)
        return pltpu.make_async_copy(tiles_hbm.at[part], tiles.at[part], sem.at[step])

    perm_copy = pltpu.make_async_copy(perm_hbm, perm, small.at[0])
    pos_copy = pltpu.make_async_copy(pos_hbm, pos, small.at[1])
    feats_copy = pltpu.make_async_copy(feats_hbm, feats, small.at[2])
    pos_copy.start()
    perm_copy.start()
    live_count = count[0, 0]

    @pl.loop(0, steps)
    def _(step):
        @pl.when(step * CHUNK < live_count)
        def _():
            chunk_copy(step).start()

    feats_copy.start()
    tiles[256] = jnp.zeros((128, 128), BF16)
    row, col, core = lax.axis_index(ROW), lax.axis_index(COL), lax.axis_index("core")
    perm_copy.wait()
    pos_copy.wait()
    own_row = jnp.zeros((1, 256), jnp.int32)
    own_col = jnp.zeros((1, 256), jnp.int32)
    for v in range(8):
        own_row += jnp.where(pos[0:1, :] == v, perm[row * 8 + v] - row * 8, 0)
    for v in range(32):
        own_col += jnp.where(pos[1:2, :] == v, perm[col * 32 + v] - col * 32, 0)
    place = (own_col >> 1) + 16 * ((own_col & 1) ^ core)
    slot = lax.broadcasted_iota(jnp.int32, (1, 256), 1)
    place = jnp.where(slot < live_count, place, 512)
    dense = own_row * 32 + place
    match = lax.broadcasted_iota(jnp.int32, (256, 256), 0) == dense
    number = lax.broadcasted_iota(jnp.int32, (16, 256), 1) + 1
    found = lax.dot_general(
        number.astype(F32).astype(BF16),
        match.astype(F32).astype(BF16),
        (((1,), (1,)), ((), ())),
        preferred_element_type=F32,
    )
    found = found[0:1, :].astype(jnp.int32)
    places[...] = jnp.where(found == 0, 256, found - 1)
    slot_copy = pltpu.make_async_copy(places, slot_ref, small.at[3])
    slot_copy.start()

    @pl.loop(0, steps)
    def _(step):
        base = step * CHUNK

        @pl.when(base < live_count)
        def _():
            chunk_copy(step).wait()
            for group in range(CHUNK // 8):
                rows = []
                for u in range(8):
                    tile = tiles[base + group * 8 + u].astype(F32)
                    rows.append(jnp.sum(tile, axis=0, keepdims=True))
                sums[pl.ds(base + group * 8, 8), :] = jnp.concatenate(rows, axis=0)

        @pl.when(base >= live_count)
        def _():
            sums[pl.ds(base, CHUNK), :] = jnp.zeros((CHUNK, 128), F32)

    pick = (lax.broadcasted_iota(jnp.int32, (32, 256), 0) == place).astype(F32).astype(BF16)
    high = sums[...].astype(BF16)
    low = (sums[...] - high.astype(F32)).astype(BF16)
    col_part = jnp.dot(pick, high, preferred_element_type=F32)
    col_part += jnp.dot(pick, low, preferred_element_type=F32)
    slot_copy.wait()
    feats_copy.wait()
    for m in range(16):
        send_ref[m, 0:128, :] = feats[...]
        send_ref[m, 128:160, :] = col_part.astype(BF16)


def degrees(*arrays):
    vmem = pl.BlockSpec(memory_space=pltpu.VMEM)
    hbm = pl.BlockSpec(memory_space=pltpu.HBM)
    return pl.pallas_call(
        degree_kernel,
        in_specs=[pl.BlockSpec(memory_space=pltpu.SMEM)] + [hbm] * 4,
        out_specs=[vmem, pl.BlockSpec(memory_space=pltpu.SMEM), vmem],
        scratch_shapes=[
            pltpu.SMEM((256,), jnp.int32),
            pltpu.VMEM((2, 256), jnp.int32),
            pltpu.VMEM((128, 128), BF16),
            pltpu.VMEM((256, 128), F32),
            pltpu.VMEM((1, 256), jnp.int32),
            pltpu.SemaphoreType.DMA((256 // CHUNK,)),
            pltpu.SemaphoreType.DMA((4,)),
        ],
        out_shape=[
            jax.ShapeDtypeStruct((16, 160, 128), BF16),
            pltpu.SMEM((1, 256), jnp.int32),
            pltpu.VMEM((257, 128, 128), BF16),
        ],
        compiler_params=pltpu.CompilerParams(vmem_limit_bytes=16 << 20),
        name="degrees",
    )(*arrays)


def row_sum_kernel(slots, tiles, sums_ref, highs, lows):
    ones = jnp.ones((16, 128), BF16)

    @pl.loop(0, 8)
    def _(i):
        total = jnp.zeros((128, 128), F32)
        for place in range(0, 32, 2):
            one, two = slots[0, i * 32 + place], slots[0, i * 32 + place + 1]
            total += (tiles[one] + tiles[two]).astype(F32)
        high = total.astype(BF16)
        rows = pl.ds(pl.multiple_of(i * 128, 128), 128)
        highs[rows, :] = high
        lows[rows, :] = (total - high.astype(F32)).astype(BF16)

    dims = (((1,), (1,)), ((), ()))
    sums = lax.dot_general(ones, highs[...], dims, preferred_element_type=F32)
    sums += lax.dot_general(ones, lows[...], dims, preferred_element_type=F32)
    high = sums.astype(BF16)
    low = (sums - high.astype(F32)).astype(BF16)
    for i in range(8):
        lanes = slice(i * 128, i * 128 + 128)
        sums_ref[i] = jnp.concatenate([high[0:8, lanes], low[0:8, lanes]], axis=0)


def row_sums(slots, tiles):
    vmem = pl.BlockSpec(memory_space=pltpu.VMEM)
    return pl.pallas_call(
        row_sum_kernel,
        in_specs=[pl.BlockSpec(memory_space=pltpu.SMEM), vmem],
        out_specs=vmem,
        out_shape=pltpu.VMEM((8, 16, 128), BF16),
        scratch_shapes=[pltpu.VMEM((1024, 128), BF16), pltpu.VMEM((1024, 128), BF16)],
        cost_estimate=pl.CostEstimate(flops=0, bytes_accessed=6 << 20, transcendentals=0),
        compiler_params=pltpu.CompilerParams(vmem_limit_bytes=16 << 20),
        name="row_sums",
    )(slots, tiles)


def product_kernel(slots, recv_a, recv_b, tiles, sums, out, rhs, acc):
    from_a = jnp.sum(recv_a[:, 128:160, :].astype(F32), axis=0)
    from_b = jnp.sum(recv_b[:, 128:160, :].astype(F32), axis=0)
    degree = 1.0 + from_a + jnp.concatenate([from_b[16:32], from_b[0:16]], axis=0)
    scale = jnp.concatenate([lax.rsqrt(degree), jnp.zeros((96, 128), F32)], axis=0).T
    for part in range(4):
        for b in range(part * 8, part * 8 + 8):
            feat = recv_a[b, 0:128, :] if b < 16 else recv_b[b - 16, 0:128, :]
            scaled = scale[:, b : b + 1] * feat.astype(F32)
            rhs[b * 128 : b * 128 + 128, :] = scaled.astype(BF16)
        dense = jnp.concatenate(
            [
                jnp.concatenate(
                    [tiles[slots[0, i * 32 + part * 8 + q]] for q in range(8)], axis=1
                )
                for i in range(8)
            ],
            axis=0,
        )
        term = jnp.dot(
            dense, rhs[part * 1024 : part * 1024 + 1024, :], preferred_element_type=F32
        )
        if part == 0:
            acc[...] = term
        elif part < 3:
            acc[...] += term
        else:
            total = (acc[...] + term).astype(BF16)
    for i in range(8):
        out[i, 0:128, :] = total[i * 128 : i * 128 + 128, :]
        out[i, 128:144, :] = sums[i]


def product(slots, recv_a, recv_b, tiles, sums):
    vmem = pl.BlockSpec(memory_space=pltpu.VMEM)
    return pl.pallas_call(
        product_kernel,
        in_specs=[pl.BlockSpec(memory_space=pltpu.SMEM), vmem, vmem, vmem, vmem],
        out_specs=vmem,
        scratch_shapes=[pltpu.VMEM((4096, 128), BF16), pltpu.VMEM((1024, 128), F32)],
        out_shape=jax.ShapeDtypeStruct((8, 144, 128), BF16),
        compiler_params=pltpu.CompilerParams(vmem_limit_bytes=24 << 20),
        name="product",
    )(slots, recv_a, recv_b, tiles, sums)


def node_kernel(parts, weight, bias, cotangent, hidden_ref, terms_ref):
    total = jnp.sum(parts[...].astype(F32), axis=0)
    row_degree = jnp.broadcast_to(1.0 + total[128:129, :] + total[136:137, :], (128, 128)).T
    aggregated = (lax.rsqrt(row_degree) * total[0:128, :]).astype(BF16)
    preact = jnp.dot(aggregated, weight[...], preferred_element_type=F32) + bias[...]
    logistic = jax.nn.sigmoid(preact)
    hidden_ref[...] = (preact * logistic).astype(BF16)
    grad = (
        cotangent[...].astype(F32) * logistic * (1.0 + preact * (1.0 - logistic))
    ).astype(BF16)
    weight_part = lax.dot_general(
        aggregated, grad, (((0,), (0,)), ((), ())), preferred_element_type=F32
    )
    bias_part = jnp.sum(grad.astype(F32), axis=0, keepdims=True)
    for k in range(16):
        for half in range(2):
            for f in range(8):
                terms_ref[k, half * 8 + f, :, :] = weight_part[
                    k * 8 + f : k * 8 + f + 1, half * 128 : half * 128 + 128
                ]
        terms_ref[k, 16, :, :] = (
            bias_part[:, k * 128 : k * 128 + 128] if k < 2 else jnp.zeros((1, 128), F32)
        )


def nodes(parts, weight, bias, cotangent):
    return pl.pallas_call(
        node_kernel,
        out_shape=[
            pltpu.VMEM((128, 256), BF16),
            jax.ShapeDtypeStruct((16, 17, 1, 128), F32),
        ],
        compiler_params=pltpu.CompilerParams(vmem_limit_bytes=16 << 20),
        name="nodes",
    )(parts, weight, bias, cotangent)


def finish_kernel(every, hidden, hidden_ref, weight_ref, bias_ref):
    hidden_ref[...] = hidden[...]
    for k in range(16):
        for half in range(2):
            for f in range(8):
                weight_ref[k * 8 + f : k * 8 + f + 1, half * 128 : half * 128 + 128] = every[
                    k, half * 8 + f, :, :
                ]
    for k in range(2):
        bias_ref[:, k * 128 : k * 128 + 128] = every[k, 16, :, :]


def finish(every, hidden):
    return pl.pallas_call(
        finish_kernel,
        out_shape=[
            jax.ShapeDtypeStruct((128, 256), BF16),
            jax.ShapeDtypeStruct((128, 256), F32),
            jax.ShapeDtypeStruct((1, 256), F32),
        ],
        compiler_params=pltpu.CompilerParams(vmem_limit_bytes=16 << 20),
        name="finish",
    )(every, hidden)


def gather(x, axes, count):
    return lax.all_to_all(jnp.broadcast_to(x[None], (count,) + x.shape), axes, 0, 0)


def body(features, weight, bias, cotangent, tile_values, tile_pos, tile_count, block_perm):
    packed = tile_values[0, 0]
    in_hbm = [
        pltpu.with_memory_space_constraint(x, pltpu.HBM)
        for x in (block_perm, tile_pos[0, 0], features, packed)
    ]
    send, slots, held = degrees(tile_count, *in_hbm)
    recv_a = lax.all_to_all(send, SAME_CORE_ROW, 0, 0)
    recv_b = lax.ppermute(recv_a, "core", SWAP)
    partial = product(slots, recv_a, recv_b, held, row_sums(slots, held))
    received = lax.all_to_all(partial, COL, 0, 0)
    hidden, terms = nodes(received, weight, bias[None], cotangent)
    own_terms = jnp.sum(lax.all_to_all(terms, NEAR, 0, 0), axis=0)
    total = jnp.sum(gather(own_terms, FAR, 16), axis=0) * lax.rsqrt(F32(32768.0))
    hidden, weight_grad, bias_grad = finish(gather(total, NEAR, 16), hidden)
    return hidden, weight_grad, bias_grad[0]


def solution(mesh):
    split = Mesh(mesh.devices.reshape(8, 2, 2, 2, 4), ("z", "y_lo", "core", "y_hi", "x"))
    placed = (
        P(COL + ROW, None),
        P(),
        P(),
        P(ROW + COL, None),
        P(ROW, COL, None, None, None),
        P(ROW, COL, None, None),
        P(ROW, COL),
        P(),
    )
    return jax.shard_map(
        body,
        mesh=split,
        in_specs=placed,
        out_specs=(P(ROW + COL, None), P(), P()),
        check_vma=False,
    )
```

```python
import functools

import jax
import jax.numpy as jnp
from jax import lax
from jax.experimental import pallas as pl
from jax.experimental.pallas import tpu as pltpu
from jax.sharding import Mesh, PartitionSpec as P

ROW = ("z", "y_lo", "core")
COL = ("y_hi", "x")
SAME_CORE_ROW = ("z", "y_lo")
NEAR = ("y_lo", "core", "x")
FAR = ("z", "y_hi")
SWAP = [(0, 1), (1, 0)]
CHUNK = 16
F32 = jnp.float32
BF16 = jnp.bfloat16


def degree_kernel(
    count, perm_hbm, pos_hbm, feats_hbm, tiles_hbm, send_ref, slot_ref, tiles,
    perm, pos, feats, sums, places, sem, small,
):
    steps = 256 // CHUNK

    def chunk_copy(step):
        part = pl.ds(step * CHUNK, CHUNK)
        return pltpu.make_async_copy(tiles_hbm.at[part], tiles.at[part], sem.at[step])

    perm_copy = pltpu.make_async_copy(perm_hbm, perm, small.at[0])
    pos_copy = pltpu.make_async_copy(pos_hbm, pos, small.at[1])
    feats_copy = pltpu.make_async_copy(feats_hbm, feats, small.at[2])
    pos_copy.start()
    perm_copy.start()
    live_count = count[0, 0]

    @pl.loop(0, steps)
    def _(step):
        @pl.when(step * CHUNK < live_count)
        def _():
            chunk_copy(step).start()

    feats_copy.start()
    tiles[256] = jnp.zeros((128, 128), BF16)
    row, col, core = lax.axis_index(ROW), lax.axis_index(COL), lax.axis_index("core")
    perm_copy.wait()
    pos_copy.wait()
    own_row = jnp.zeros((1, 256), jnp.int32)
    own_col = jnp.zeros((1, 256), jnp.int32)
    for v in range(8):
        own_row += jnp.where(pos[0:1, :] == v, perm[row * 8 + v] - row * 8, 0)
    for v in range(32):
        own_col += jnp.where(pos[1:2, :] == v, perm[col * 32 + v] - col * 32, 0)
    place = (own_col >> 1) + 16 * ((own_col & 1) ^ core)
    slot = lax.broadcasted_iota(jnp.int32, (1, 256), 1)
    place = jnp.where(slot < live_count, place, 512)
    dense = own_row * 32 + place
    match = lax.broadcasted_iota(jnp.int32, (256, 256), 0) == dense
    number = lax.broadcasted_iota(jnp.int32, (16, 256), 1) + 1
    found = lax.dot_general(
        number.astype(F32).astype(BF16),
        match.astype(F32).astype(BF16),
        (((1,), (1,)), ((), ())),
        preferred_element_type=F32,
    )
    found = found[0:1, :].astype(jnp.int32)
    places[...] = jnp.where(found == 0, 256, found - 1)
    slot_copy = pltpu.make_async_copy(places, slot_ref, small.at[3])
    slot_copy.start()

    @pl.loop(0, steps)
    def _(step):
        base = step * CHUNK

        @pl.when(base < live_count)
        def _():
            chunk_copy(step).wait()
            for group in range(CHUNK // 8):
                rows = []
                for u in range(8):
                    tile = tiles[base + group * 8 + u].astype(F32)
                    rows.append(jnp.sum(tile, axis=0, keepdims=True))
                sums[pl.ds(base + group * 8, 8), :] = jnp.concatenate(rows, axis=0)

        @pl.when(base >= live_count)
        def _():
            sums[pl.ds(base, CHUNK), :] = jnp.zeros((CHUNK, 128), F32)

    pick = (lax.broadcasted_iota(jnp.int32, (32, 256), 0) == place).astype(F32).astype(BF16)
    high = sums[...].astype(BF16)
    low = (sums[...] - high.astype(F32)).astype(BF16)
    col_part = jnp.dot(pick, high, preferred_element_type=F32)
    col_part += jnp.dot(pick, low, preferred_element_type=F32)
    slot_copy.wait()
    feats_copy.wait()
    turned = feats[...].astype(F32).T.astype(BF16)
    for m in range(16):
        send_ref[m, 0:128, :] = turned
        send_ref[m, 128:160, :] = col_part.astype(BF16)


def degrees(*arrays):
    vmem = pl.BlockSpec(memory_space=pltpu.VMEM)
    hbm = pl.BlockSpec(memory_space=pltpu.HBM)
    return pl.pallas_call(
        degree_kernel,
        in_specs=[pl.BlockSpec(memory_space=pltpu.SMEM)] + [hbm] * 4,
        out_specs=[vmem, pl.BlockSpec(memory_space=pltpu.SMEM), vmem],
        scratch_shapes=[
            pltpu.SMEM((256,), jnp.int32),
            pltpu.VMEM((2, 256), jnp.int32),
            pltpu.VMEM((128, 128), BF16),
            pltpu.VMEM((256, 128), F32),
            pltpu.VMEM((1, 256), jnp.int32),
            pltpu.SemaphoreType.DMA((256 // CHUNK,)),
            pltpu.SemaphoreType.DMA((4,)),
        ],
        out_shape=[
            jax.ShapeDtypeStruct((16, 160, 128), BF16),
            pltpu.SMEM((1, 256), jnp.int32),
            pltpu.VMEM((257, 128, 128), BF16),
        ],
        compiler_params=pltpu.CompilerParams(vmem_limit_bytes=16 << 20),
        name="degrees",
    )(*arrays)


def row_sum_kernel(slots, tiles, sums_ref, highs, lows):
    ones = jnp.ones((16, 128), BF16)

    @pl.loop(0, 8)
    def _(i):
        total = jnp.zeros((128, 128), F32)
        for place in range(0, 32, 2):
            one, two = slots[0, i * 32 + place], slots[0, i * 32 + place + 1]
            total += (tiles[one] + tiles[two]).astype(F32)
        high = total.astype(BF16)
        rows = pl.ds(pl.multiple_of(i * 128, 128), 128)
        highs[rows, :] = high
        lows[rows, :] = (total - high.astype(F32)).astype(BF16)

    dims = (((1,), (1,)), ((), ()))
    sums = lax.dot_general(ones, highs[...], dims, preferred_element_type=F32)
    sums += lax.dot_general(ones, lows[...], dims, preferred_element_type=F32)
    high = sums.astype(BF16)
    low = (sums - high.astype(F32)).astype(BF16)
    for i in range(8):
        lanes = slice(i * 128, i * 128 + 128)
        sums_ref[i] = jnp.concatenate([high[0:8, lanes], low[0:8, lanes]], axis=0)


def row_sums(slots, tiles):
    vmem = pl.BlockSpec(memory_space=pltpu.VMEM)
    return pl.pallas_call(
        row_sum_kernel,
        in_specs=[pl.BlockSpec(memory_space=pltpu.SMEM), vmem],
        out_specs=vmem,
        out_shape=pltpu.VMEM((8, 16, 128), BF16),
        scratch_shapes=[pltpu.VMEM((1024, 128), BF16), pltpu.VMEM((1024, 128), BF16)],
        cost_estimate=pl.CostEstimate(flops=0, bytes_accessed=6 << 20, transcendentals=0),
        compiler_params=pltpu.CompilerParams(vmem_limit_bytes=16 << 20),
        name="row_sums",
    )(slots, tiles)


def product_kernel(slots, recv_a, recv_b, tiles, sums, out, lhs, acc):
    from_a = jnp.sum(recv_a[:, 128:160, :].astype(F32), axis=0)
    from_b = jnp.sum(recv_b[:, 128:160, :].astype(F32), axis=0)
    degree = 1.0 + from_a + jnp.concatenate([from_b[16:32], from_b[0:16]], axis=0)
    scale = lax.rsqrt(degree)
    for part in range(4):
        for b in range(part * 8, part * 8 + 8):
            feat = recv_a[b, 0:128, :] if b < 16 else recv_b[b - 16, 0:128, :]
            scaled = scale[b : b + 1, :] * feat.astype(F32)
            lhs[part, :, b % 8 * 128 : b % 8 * 128 + 128] = scaled.astype(BF16)
        dense = jnp.concatenate(
            [
                jnp.concatenate(
                    [tiles[slots[0, i * 32 + part * 8 + q]] for q in range(8)], axis=1
                )
                for i in range(8)
            ],
            axis=0,
        )
        term = lax.dot_general(
            lhs[part], dense, (((1,), (1,)), ((), ())), preferred_element_type=F32
        )
        if part == 0:
            acc[...] = term
        elif part < 3:
            acc[...] += term
        else:
            total = (acc[...] + term).astype(BF16)
    for i in range(8):
        out[i, 0:128, :] = total[:, i * 128 : i * 128 + 128]
        out[i, 128:144, :] = sums[i]


def product(slots, recv_a, recv_b, tiles, sums):
    vmem = pl.BlockSpec(memory_space=pltpu.VMEM)
    return pl.pallas_call(
        product_kernel,
        in_specs=[pl.BlockSpec(memory_space=pltpu.SMEM), vmem, vmem, vmem, vmem],
        out_specs=vmem,
        scratch_shapes=[pltpu.VMEM((4, 128, 1024), BF16), pltpu.VMEM((128, 1024), F32)],
        out_shape=jax.ShapeDtypeStruct((8, 144, 128), BF16),
        compiler_params=pltpu.CompilerParams(vmem_limit_bytes=24 << 20),
        name="product",
    )(slots, recv_a, recv_b, tiles, sums)


def node_kernel(parts, weight, bias, cotangent, hidden_ref, terms_ref):
    total = jnp.sum(parts[...].astype(F32), axis=0)
    row_degree = 1.0 + total[128:129, :] + total[136:137, :]
    aggregated = (lax.rsqrt(row_degree) * total[0:128, :]).astype(BF16)
    preact = lax.dot_general(
        aggregated, weight[...], (((0,), (0,)), ((), ())), preferred_element_type=F32
    )
    preact += bias[...]
    logistic = jax.nn.sigmoid(preact)
    hidden_ref[...] = (preact * logistic).astype(BF16)
    grad = (
        cotangent[...].astype(F32) * logistic * (1.0 + preact * (1.0 - logistic))
    ).astype(BF16)
    weight_part = jnp.dot(aggregated, grad, preferred_element_type=F32)
    bias_part = jnp.sum(grad.astype(F32), axis=0, keepdims=True)
    for k in range(16):
        for half in range(2):
            for f in range(8):
                terms_ref[k, half * 8 + f, :, :] = weight_part[
                    k * 8 + f : k * 8 + f + 1, half * 128 : half * 128 + 128
                ]
        terms_ref[k, 16, :, :] = (
            bias_part[:, k * 128 : k * 128 + 128] if k < 2 else jnp.zeros((1, 128), F32)
        )


def nodes(parts, weight, bias, cotangent):
    return pl.pallas_call(
        node_kernel,
        out_shape=[
            pltpu.VMEM((128, 256), BF16),
            jax.ShapeDtypeStruct((16, 17, 1, 128), F32),
        ],
        compiler_params=pltpu.CompilerParams(vmem_limit_bytes=16 << 20),
        name="nodes",
    )(parts, weight, bias, cotangent)


def finish_kernel(every, hidden, hidden_ref, weight_ref, bias_ref):
    hidden_ref[...] = hidden[...]
    for k in range(16):
        for half in range(2):
            for f in range(8):
                weight_ref[k * 8 + f : k * 8 + f + 1, half * 128 : half * 128 + 128] = every[
                    k, half * 8 + f, :, :
                ]
    for k in range(2):
        bias_ref[:, k * 128 : k * 128 + 128] = every[k, 16, :, :]


def finish(every, hidden):
    return pl.pallas_call(
        finish_kernel,
        out_shape=[
            jax.ShapeDtypeStruct((128, 256), BF16),
            jax.ShapeDtypeStruct((128, 256), F32),
            jax.ShapeDtypeStruct((1, 256), F32),
        ],
        compiler_params=pltpu.CompilerParams(vmem_limit_bytes=16 << 20),
        name="finish",
    )(every, hidden)


def gather(x, axes, count):
    return lax.all_to_all(jnp.broadcast_to(x[None], (count,) + x.shape), axes, 0, 0)


def body(features, weight, bias, cotangent, tile_values, tile_pos, tile_count, block_perm):
    packed = tile_values[0, 0]
    in_hbm = [
        pltpu.with_memory_space_constraint(x, pltpu.HBM)
        for x in (block_perm, tile_pos[0, 0], features, packed)
    ]
    send, slots, held = degrees(tile_count, *in_hbm)
    recv_a = lax.all_to_all(send, SAME_CORE_ROW, 0, 0)
    recv_b = lax.ppermute(recv_a, "core", SWAP)
    partial = product(slots, recv_a, recv_b, held, row_sums(slots, held))
    received = lax.all_to_all(partial, COL, 0, 0)
    hidden, terms = nodes(received, weight, bias[None], cotangent)
    own_terms = jnp.sum(lax.all_to_all(terms, NEAR, 0, 0), axis=0)
    total = jnp.sum(gather(own_terms, FAR, 16), axis=0) * lax.rsqrt(F32(32768.0))
    hidden, weight_grad, bias_grad = finish(gather(total, NEAR, 16), hidden)
    return hidden, weight_grad, bias_grad[0]


def solution(mesh):
    split = Mesh(mesh.devices.reshape(8, 2, 2, 2, 4), ("z", "y_lo", "core", "y_hi", "x"))
    placed = (
        P(COL + ROW, None),
        P(),
        P(),
        P(ROW + COL, None),
        P(ROW, COL, None, None, None),
        P(ROW, COL, None, None),
        P(ROW, COL),
        P(),
    )
    return jax.shard_map(
        body,
        mesh=split,
        in_specs=placed,
        out_specs=(P(ROW + COL, None), P(), P()),
        check_vma=False,
    )
```
